32 devices in a mesh: ctx: 8 (over z, core), hid: 4 (over y, x).
Axes of the slice: x: 2, y: 2, z: 4, core: 2. Of those that a mesh axis runs over, the one named last changes fastest.
Arguments:
- tokens: bfloat16 [1, 32768, 4096], P(None, 'ctx', 'hid'), may hold values from -40 to 40
- seq_inner: bfloat16 [256, 256], replicated, may hold values from -0.375 to 0.375
- seq_outer: bfloat16 [128, 128], replicated, may hold values from -0.5 to 0.5
- inv_outer: bfloat16 [128, 128], replicated, may hold values from -0.5 to 0.5
- inv_inner: bfloat16 [256, 256], replicated, may hold values from -0.375 to 0.375
- twiddle_in: float32 [128, 256], P('ctx'), may hold values from -1.7 to 1.7
- twiddle_out: float32 [128, 256], P(None, 'ctx'), may hold values from -1.7 to 1.7
- freq_kernel: bfloat16 [128, 256, 4096], P('ctx', None, 'hid'), may hold values from -4 to 4
- first_gain: float32 [4096], P('hid'), may hold values from 0.25 to 1.75
- second_gain: float32 [4096], P('hid'), may hold values from 0.25 to 1.75
- right_up: bfloat16 [64, 64, 64], P('hid'), may hold values from -0.75 to 0.75
- left_up: bfloat16 [64, 64, 128], P('hid'), may hold values from -0.75 to 0.75
- right_down: bfloat16 [64, 128, 64], P('hid'), may hold values from -0.5 to 0.5
- left_down: bfloat16 [64, 64, 64], P('hid'), may hold values from -0.75 to 0.75
Outputs:
- block_out: bfloat16 [1, 32768, 4096], P(None, 'ctx', 'hid')
The draws below stay inside these ranges and needn't reach their ends.
All inputs are finite; a program needn't handle non-finite values.
Results may differ from the reference program's by a relative error of at most 0.0085.
Values may be sent and summed in bfloat16 or wider, within the bound.
No kernel may reach another device: no remote copies, remote signals or barrier semaphores. Data moves between devices by JAX's collectives and lax.ppermute only.
A program may use at most 192 MiB of HBM per device.

```python
from functools import partial
import jax
import jax.numpy as jnp
from jax import lax

SA = 128
SB = 256
SEQ = 32768
NB = 64
D = 4096
MF = 128
BATCH = 1


def draw_tokens(key, part):
    k_base, k_col, k_row = jax.random.split(key, 3)
    column = jnp.arange(D, dtype=jnp.float32) / (D - 1)
    base_draw = jax.random.truncated_normal(k_base, -4.0, 4.0, (BATCH, SEQ, D), jnp.float32)
    column_ramp = 1.8 ** (column - 0.5)
    jitter = jnp.exp(jax.random.uniform(k_col, (D,), jnp.float32, -0.35, 0.35))
    row_scale = jnp.exp(jax.random.uniform(k_row, (BATCH, SEQ, 1), jnp.float32, -0.5, 0.5))
    return (base_draw * column_ramp * jitter * row_scale).astype(jnp.bfloat16)


def levels(key, extent, cuts, low, top_value):
    def one(dim, parts):
        draws = jax.random.uniform(jax.random.fold_in(jax.random.fold_in(key, 6), dim), (parts,), jnp.float32, low / len(cuts), top_value / len(cuts))
        return jnp.repeat(jnp.exp(draws), extent[dim] // parts).reshape((-1,) + (1,) * (len(extent) - dim - 1))

    loudness = one(*cuts[0])
    for cut in cuts[1:]:
        loudness = loudness * one(*cut)
    return loudness


def noise(stream_key, dims, deviation, limit, cuts=(), kind=jnp.bfloat16):
    array = jax.random.normal(stream_key, dims, jnp.float32) * deviation
    if len(cuts) > 0:
        array = levels(stream_key, dims, cuts, -0.22, 0.18) * array
    return jnp.clip(array, min=-limit, max=limit).astype(kind)


def setup_inputs(seed: int = 0) -> dict:
    streams_of = jax.random.split(jax.random.key(seed), 15)
    tokens = draw_tokens(jax.random.fold_in(streams_of[14], 71), 0)
    seq_inner = noise(streams_of[1], (SB, SB), SB ** -0.5, 0.375)
    seq_outer = noise(streams_of[2], (SA, SA), SA ** -0.5, 0.5)
    inv_outer = noise(streams_of[3], (SA, SA), SA ** -0.5, 0.5)
    inv_inner = noise(streams_of[4], (SB, SB), SB ** -0.5, 0.375)
    twiddle_in = jnp.clip(jax.random.uniform(streams_of[5], (SA, SB), jnp.float32, -1.7, 1.7) * levels(streams_of[5], (SA, SB), ((0, 8),), -0.4, 0.0), -1.7, 1.7)
    twiddle_out = jnp.clip(jax.random.uniform(streams_of[6], (SA, SB), jnp.float32, -1.7, 1.7) * levels(streams_of[6], (SA, SB), ((1, 8),), -0.4, 0.0), -1.7, 1.7)
    freq_kernel = noise(streams_of[7], (SA, SB, D), 1.0, 4.0, ((0, 8), (2, 4)))
    first_gain = jnp.clip(1.0 + 0.15 * jax.random.normal(streams_of[8], (D,), jnp.float32), 0.25, 1.75)
    second_gain = jnp.clip(1.0 + 0.15 * jax.random.normal(streams_of[9], (D,), jnp.float32), 0.25, 1.75)
    right_up = noise(streams_of[10], (NB, NB, NB), NB ** -0.5, 0.75, ((0, 4),))
    left_up = noise(streams_of[11], (NB, NB, MF), NB ** -0.5, 0.75, ((0, 4),))
    right_down = noise(streams_of[12], (NB, MF, NB), MF ** -0.5, 0.5, ((0, 4),))
    left_down = noise(streams_of[13], (NB, NB, NB), NB ** -0.5, 0.75, ((0, 4),))
    return dict(tokens=tokens, seq_inner=seq_inner, seq_outer=seq_outer, inv_outer=inv_outer, inv_inner=inv_inner, twiddle_in=twiddle_in, twiddle_out=twiddle_out, freq_kernel=freq_kernel, first_gain=first_gain, second_gain=second_gain, right_up=right_up, left_up=left_up, right_down=right_down, left_down=left_down)


EPS = 1e-06

def seq_filter(pieces, seq_inner, seq_outer, inv_outer, inv_inner, twiddle_in, twiddle_out):
    normed_grid, kern_grid = pieces
    inner_mix = jnp.einsum('qb,abc->aqc', seq_inner.astype(jnp.float32), normed_grid.astype(jnp.float32))
    inner_mix = lax.optimization_barrier((inner_mix * twiddle_in[:, :, None]).astype(jnp.bfloat16))
    outer_mix = jnp.einsum('pa,aqc->pqc', seq_outer.astype(jnp.float32), inner_mix.astype(jnp.float32))
    outer_mix = lax.optimization_barrier(outer_mix.astype(jnp.bfloat16))
    filtered = lax.optimization_barrier((outer_mix.astype(jnp.float32) * kern_grid.astype(jnp.float32)).astype(jnp.bfloat16))
    backed = jnp.einsum('rp,pqc->rqc', inv_outer.astype(jnp.float32), filtered.astype(jnp.float32))
    backed = lax.optimization_barrier((backed * twiddle_out[:, :, None]).astype(jnp.bfloat16))
    return jnp.einsum('eq,rqc->rec', inv_inner.astype(jnp.float32), backed.astype(jnp.float32))

def mlp_block(block_rows, second_gain, right_up, left_up, right_down, left_down):
    count = block_rows.shape[0]
    sumsq = lax.optimization_barrier(jnp.sum(block_rows * block_rows, axis=-1, keepdims=True))
    normed_two = (block_rows * (second_gain * lax.rsqrt(sumsq / D + EPS))).astype(jnp.bfloat16)
    normed_two = lax.optimization_barrier(normed_two)
    projected = jnp.einsum('tij,ijk->tik', normed_two.reshape(count, NB, NB).astype(jnp.float32), right_up.astype(jnp.float32))
    projected = lax.optimization_barrier(projected.astype(jnp.bfloat16))
    hidden = jnp.einsum('tik,kim->tkm', projected.astype(jnp.float32), left_up.astype(jnp.float32))
    active = lax.optimization_barrier(jax.nn.gelu(hidden, approximate=True).astype(jnp.bfloat16))
    reduced = jnp.einsum('tkm,kmq->tkq', active.astype(jnp.float32), right_down.astype(jnp.float32))
    reduced = lax.optimization_barrier(reduced.astype(jnp.bfloat16))
    result = jnp.einsum('tkq,qkr->tqr', reduced.astype(jnp.float32), left_down.astype(jnp.float32))
    return (block_rows + result.reshape(count, D)).astype(jnp.bfloat16)

def reference(tokens, seq_inner, seq_outer, inv_outer, inv_inner, twiddle_in, twiddle_out, freq_kernel, first_gain, second_gain, right_up, left_up, right_down, left_down):
    wide = tokens.astype(jnp.float32)
    first_sums = lax.optimization_barrier(jnp.sum(wide * wide, axis=-1, keepdims=True))
    normed = (wide * (first_gain * lax.rsqrt(first_sums / D + EPS))).astype(jnp.bfloat16)
    normed = lax.optimization_barrier(normed)
    groups = 8
    chans = D // groups
    grid = normed.reshape(BATCH, SA, SB, groups, chans).transpose(0, 3, 1, 2, 4).reshape(BATCH * groups, SA, SB, chans)
    kern_split = freq_kernel.reshape(SA, SB, groups, chans).transpose(2, 0, 1, 3)
    kern_all = jnp.broadcast_to(kern_split[None], (BATCH, groups, SA, SB, chans)).reshape(BATCH * groups, SA, SB, chans)
    filter_fn = partial(seq_filter, seq_inner=seq_inner, seq_outer=seq_outer, inv_outer=inv_outer, inv_inner=inv_inner, twiddle_in=twiddle_in, twiddle_out=twiddle_out)
    conv = lax.map(filter_fn, (grid, kern_all))
    conv = conv.reshape(BATCH, groups, SEQ, chans).transpose(0, 2, 1, 3).reshape(BATCH, SEQ, D)
    mixed = wide + conv * jax.nn.silu(normed.astype(jnp.float32))
    blocks = 16
    block_fn = partial(mlp_block, second_gain=second_gain, right_up=right_up, left_up=left_up, right_down=right_down, left_down=left_down)
    output = lax.map(block_fn, mixed.reshape(blocks, BATCH * SEQ // blocks, D))
    return output.reshape(BATCH, SEQ, D)
```

```python
import math

import jax
import jax.numpy as jnp
from jax import lax
from jax.experimental import pallas as pl
from jax.experimental.pallas import tpu as pltpu
from jax.sharding import PartitionSpec as P

EPS = 1e-06
G = 16
ROWS = 256
BF = jnp.bfloat16
F32 = jnp.float32

RETURN_SPLIT = (4, 4, 4, 2, 2)
CHANNEL_SPLIT = (3, 1)


def cost(flops, moved, exps=0):
    return pl.CostEstimate(flops=int(flops), bytes_accessed=int(moved), transcendentals=int(exps))


def dot(a, b):
    return jnp.dot(a, b, preferred_element_type=F32)


def whole(shape):
    zeros = (0,) * len(shape)
    return pl.BlockSpec(shape, lambda *_: zeros, pipeline_mode=pl.Buffered(1))


def xor_blocks(x, axis, me, parts):
    size = x.shape[axis] // parts
    return jnp.concatenate(
        [lax.dynamic_slice_in_dim(x, (me ^ d) * size, size, axis) for d in range(parts)], axis
    )


def swap(x, name, size, d):
    return lax.ppermute(x, name, [(i, i ^ d) for i in range(size)])


def exchange(pieces, name, size):
    order = sorted(range(1, size), key=lambda d: -d)
    got = {d: swap(pieces[d], name, size, d) for d in order}
    return [pieces[0]] + [got[d] for d in range(1, size)]


def inner_kernel(parts, splits, tok, scale, gain, mix, twiddle, *outs):
    normed = (tok[...].astype(F32) * (gain[...] * scale[...])).astype(BF)
    mixed = (dot(mix[...], normed) * twiddle[0]).astype(BF)
    rows = mixed.shape[0] // parts
    for d in range(parts):
        start = 0
        for f, width in enumerate(splits):
            outs[f * parts + d][0] = mixed[d * rows : (d + 1) * rows, start : start + width]
            start += width


def inner(tokens, scale, gain, mix, twiddle, parts, splits):
    count, chans = tokens.shape
    block = mix.shape[0]
    rows = count // block
    ql = block // parts
    return pl.pallas_call(
        lambda *refs: inner_kernel(parts, splits, *refs),
        grid=(rows,),
        in_specs=[
            pl.BlockSpec((block, chans), lambda a: (a, 0)),
            pl.BlockSpec((block, 1), lambda a: (a, 0)),
            whole((1, chans)),
            whole((block, block)),
            pl.BlockSpec((1, block, 1), lambda a: (a, 0, 0)),
        ],
        out_specs=[
            pl.BlockSpec((1, ql, width), lambda a: (a, 0, 0)) for width in splits for _ in range(parts)
        ],
        out_shape=[
            jax.ShapeDtypeStruct((rows, ql, width), BF) for width in splits for _ in range(parts)
        ],
        cost_estimate=cost(2 * count * block * chans, 4 * count * chans),
        name="inner_mix",
    )(tokens, scale, gain, mix, twiddle)


def outer_kernel(parts, sizes, *refs):
    pieces = refs[:parts]
    kern, fwd, back, twiddle = refs[parts : parts + 4]
    outs = refs[-parts * len(sizes) :]
    width = kern.shape[-1]
    x = jnp.concatenate([p[...].reshape(-1, width) for p in pieces], axis=0)
    mixed = dot(fwd[...], x).astype(BF)
    filtered = (mixed.astype(F32) * kern[...].reshape(-1, width).astype(F32)).astype(BF)
    backed = (dot(back[...], filtered) * twiddle[0]).astype(BF)
    row = 0
    for d in range(parts):
        for j, size in enumerate(sizes):
            outs[j * parts + d][...] = backed[row * G : (row + size) * G].reshape(size, G, width)
            row += size


def outer(pieces, kern, fwd, back, twiddle, sizes, start, carried):
    parts = len(pieces)
    rows, ql, width = pieces[0].shape
    chans = kern.shape[-1]
    side = fwd.shape[0]
    cb = math.gcd(math.gcd(width, start), 256)
    first = start // cb
    aliases = {} if carried is None else {parts + 4 + i: i for i in range(len(carried))}
    extra = [] if carried is None else list(carried)
    return pl.pallas_call(
        lambda *refs: outer_kernel(parts, sizes, *refs),
        grid=(width // cb, ql // G),
        in_specs=[pl.BlockSpec((rows, G, cb), lambda c, q: (0, q, c)) for _ in range(parts)]
        + [
            pl.BlockSpec((parts, rows, G, cb), lambda c, q: (0, 0, q, c + first)),
            whole((side, side)),
            whole((side, side)),
            pl.BlockSpec((1, side, 1), lambda c, q: (q, 0, 0)),
        ]
        + [pl.BlockSpec(memory_space=pl.ANY) for _ in extra],
        out_specs=[
            pl.BlockSpec((size, G, cb), lambda c, q: (0, q, c + first)) for size in sizes for _ in range(parts)
        ],
        out_shape=[jax.ShapeDtypeStruct((size, ql, chans), BF) for size in sizes for _ in range(parts)],
        input_output_aliases=aliases,
        cost_estimate=cost(4 * side * side * ql // G * width, 6 * side * ql // G * width),
        name="outer_mix",
    )(*pieces, kern, fwd, back, twiddle, *extra)


def mix_kernel(parts, groups, *refs):
    pieces = refs[:parts]
    tok, scale, gain, gain_two, back, up = refs[parts : parts + 6]
    mixed_out = refs[parts + 6]
    outs = refs[parts + 7 :]
    home = jnp.concatenate([p[0] for p in pieces], axis=0)
    conv = dot(back[...], home)
    wide = tok[...].astype(F32)
    normed = (wide * (gain[...] * scale[...])).astype(BF).astype(F32)
    mixed = wide + conv * (normed / (1.0 + jnp.exp(-normed)))
    mixed_out[...] = mixed
    sums = jnp.sum(mixed * mixed, axis=1, keepdims=True)
    high = sums.astype(BF)
    rest = sums - high.astype(F32)
    mid = rest.astype(BF)
    low = rest - mid.astype(F32)
    lane = lax.broadcasted_iota(jnp.int32, (mixed.shape[0], 128), 1)
    tail = jnp.where(
        lane == 0,
        high.astype(F32),
        jnp.where(lane == 1, mid.astype(F32), jnp.where(lane == 2, low, 0.0)),
    ).astype(BF)
    projected = dot((mixed * gain_two[...]).astype(BF), up[...]).astype(BF)
    width = projected.shape[1] // groups
    for d in range(groups):
        outs[d][:, :width] = projected[:, d * width : (d + 1) * width]
        outs[d][:, width:] = tail


def mix(pieces, tokens, scale, gain, gain_two, back, up, row, groups):
    parts = len(pieces)
    size, ql, chans = pieces[0].shape
    block = ql * parts
    count = size * block
    width = up.shape[1] // groups
    return pl.pallas_call(
        lambda *refs: mix_kernel(parts, groups, *refs),
        grid=(size,),
        in_specs=[pl.BlockSpec((1, ql, chans), lambda r: (r, 0, 0)) for _ in range(parts)]
        + [
            pl.BlockSpec((block, chans), lambda r: (r + row, 0)),
            pl.BlockSpec((block, 1), lambda r: (r + row, 0)),
            whole((1, chans)),
            whole((1, chans)),
            whole((block, block)),
            whole(up.shape),
        ],
        out_specs=[pl.BlockSpec((block, chans), lambda r: (r, 0))]
        + [pl.BlockSpec((block, width + 128), lambda r: (r, 0)) for _ in range(groups)],
        out_shape=[jax.ShapeDtypeStruct((count, chans), F32)]
        + [jax.ShapeDtypeStruct((count, width + 128), BF) for _ in range(groups)],
        cost_estimate=cost(2 * count * chans * (block + up.shape[1]), 11 * count * chans, count * chans),
        name="mix_tokens",
    )(*pieces, tokens, scale, gain, gain_two, back, up)


def hidden_kernel(groups, total, *refs):
    pieces = refs[:groups]
    up, down = refs[groups : groups + 2]
    outs = refs[groups + 2 :]
    width = up.shape[0] // groups
    sums = sum(jnp.sum(p[:, width:].astype(F32), axis=1, keepdims=True) for p in pieces)
    scale = lax.rsqrt(sums / total + EPS)
    x = jnp.concatenate([p[:, :width] for p in pieces], axis=1)
    v = dot(x, up[...]) * scale
    active = (0.5 * v * (1.0 + jnp.tanh(0.7978845608 * (v + 0.044715 * (v * v * v))))).astype(BF)
    reduced = dot(active, down[...]).astype(BF)
    step = reduced.shape[1] // groups
    for d in range(groups):
        outs[d][...] = reduced[:, d * step : (d + 1) * step]


def hidden(pieces, up, down, total):
    groups = len(pieces)
    count, wide = pieces[0].shape
    step = down.shape[1] // groups
    tb = min(ROWS, count)
    return pl.pallas_call(
        lambda *refs: hidden_kernel(groups, total, *refs),
        grid=(count // tb,),
        in_specs=[pl.BlockSpec((tb, wide), lambda t: (t, 0)) for _ in range(groups)]
        + [whole(up.shape), whole(down.shape)],
        out_specs=[pl.BlockSpec((tb, step), lambda t: (t, 0)) for _ in range(groups)],
        out_shape=[jax.ShapeDtypeStruct((count, step), BF) for _ in range(groups)],
        cost_estimate=cost(
            2 * count * up.shape[1] * (up.shape[0] + down.shape[1]),
            2 * groups * count * (wide + step),
            count * up.shape[1],
        ),
        name="hidden_units",
    )(*pieces, up, down)


def final_kernel(groups, *refs):
    pieces = refs[:groups]
    mixed, left = refs[groups : groups + 2]
    out = refs[-1]
    x = jnp.concatenate([p[...] for p in pieces], axis=1)
    out[...] = (mixed[...] + dot(x, left[...])).astype(BF)


def final(pieces, mixed, left, row, count_all, carried):
    groups = len(pieces)
    count, step = pieces[0].shape
    chans = mixed.shape[1]
    tb = min(ROWS, count)
    first = row // tb
    extra = [] if carried is None else [carried]
    return pl.pallas_call(
        lambda *refs: final_kernel(groups, *refs),
        grid=(count // tb,),
        in_specs=[pl.BlockSpec((tb, step), lambda t: (t, 0)) for _ in range(groups)]
        + [pl.BlockSpec((tb, chans), lambda t: (t, 0)), whole(left.shape)]
        + [pl.BlockSpec(memory_space=pl.ANY) for _ in extra],
        out_specs=pl.BlockSpec((tb, chans), lambda t: (t + first, 0)),
        out_shape=jax.ShapeDtypeStruct((count_all, chans), BF),
        input_output_aliases={groups + 2: 0} if extra else {},
        cost_estimate=cost(2 * count * groups * step * chans, 8 * count * chans),
        name="block_out",
    )(*pieces, mixed, left, *extra)


def iota(shape, axis):
    return lax.broadcasted_iota(jnp.int32, shape, axis)


def pick(rows, cols, of_col):
    return (iota((rows, cols), 0) == of_col(iota((rows, cols), 1))).astype(BF)


def masked(x, keep):
    rows, cols = iota(x.shape, 0), iota(x.shape, 1)
    return jnp.where(keep(rows, cols), x, 0.0).astype(BF)


def spread_pairs(x):
    rows, cols = x.shape
    wide = dot(x, pick(cols, cols * G, lambda c: c // G))
    tall = jnp.broadcast_to(wide[:, None, :], (rows, G, cols * G)).reshape(rows * G, cols * G)
    return masked(tall, lambda r, c: r % G == c % G)


def expand_factors(right_up, left_up, right_down, left_down, me, groups):
    il, nj, nk = right_up.shape
    kl, ni, nm = left_up.shape
    nq = right_down.shape[2]
    ql, _, nr = left_down.shape
    lk, lr = kl * il, ql * kl
    up_one = masked(
        dot(
            right_up.reshape(il * nj, nk),
            pick(nk, groups * lk, lambda c: (me ^ (c // lk)) * kl + c % lk // il),
        ),
        lambda r, c: r // nj == c % il,
    )
    rows = groups * lk

    def source(r):
        return (r % lk // il) * ni + (me ^ (r // lk)) * il + r % il

    pick_rows = (source(iota((rows, kl * ni), 0)) == iota((rows, kl * ni), 1)).astype(BF)
    taken = dot(pick_rows, left_up.reshape(kl * ni, nm))
    tiled = jnp.broadcast_to(taken[:, None, :], (rows, kl, nm)).reshape(rows, kl * nm)
    up_two = masked(tiled, lambda r, c: c // nm == r % lk // il)
    down_one = masked(
        dot(
            right_down.reshape(kl * nm, nq),
            pick(nq, groups * lr, lambda c: (me ^ (c // lr)) * ql + c % lr // kl),
        ),
        lambda r, c: r // nm == c % kl,
    )
    rows = groups * lr
    nkk = left_down.shape[1]

    def source_two(r):
        return (r % lr // kl) * nkk + (me ^ (r // lr)) * kl + r % kl

    pick_rows = (source_two(iota((rows, ql * nkk), 0)) == iota((rows, ql * nkk), 1)).astype(BF)
    taken = dot(pick_rows, left_down.reshape(ql * nkk, nr)).astype(BF)
    down_two = masked(
        dot(taken, pick(nr, ql * nr, lambda c: c % nr)),
        lambda r, c: c // nr == r % lr // kl,
    )
    return up_one, up_two, down_one, down_two


def splits_of(total, shares):
    unit = total // sum(shares)
    if unit * sum(shares) != total:
        return [total]
    return [unit * share for share in shares]


def make_shards(parts, groups):
    def shards(
        tokens,
        seq_inner,
        seq_outer,
        inv_outer,
        inv_inner,
        twiddle_in,
        twiddle_out,
        freq_kernel,
        first_gain,
        second_gain,
        right_up,
        left_up,
        right_down,
        left_down,
    ):
        _, count, chans = tokens.shape
        total = chans * groups
        block = seq_inner.shape[0]
        ql = block // parts
        al = count // block
        at = lax.axis_index("ctx")
        me = lax.axis_index("hid")
        tok = tokens.reshape(count, chans)

        sent = freq_kernel.reshape(al, parts, ql, chans).transpose(1, 0, 2, 3)
        kern = lax.all_to_all(sent, "ctx", split_axis=0, concat_axis=0, tiled=True)

        wide = tok.astype(F32)
        sums = lax.psum(jnp.sum(wide * wide, axis=1), "hid")
        scale = lax.rsqrt(sums / total + EPS).reshape(count, 1)
        gain = first_gain.reshape(1, chans)
        gain_two = second_gain.reshape(1, chans)

        chan_splits = splits_of(chans, CHANNEL_SPLIT)
        mixes = inner(
            tok,
            scale,
            gain,
            xor_blocks(seq_inner, 0, at, parts),
            xor_blocks(twiddle_in, 1, at, parts).reshape(al, block, 1),
            parts,
            chan_splits,
        )

        fwd = spread_pairs(xor_blocks(seq_outer, 1, at, parts))
        back = spread_pairs(xor_blocks(inv_outer, 0, at, parts))
        side = fwd.shape[0]
        turn = xor_blocks(twiddle_out, 0, at, parts)
        turn = turn.reshape(side // G, ql // G, G).transpose(1, 0, 2).reshape(ql // G, side, 1)
        sizes = splits_of(al, RETURN_SPLIT)

        backed = None
        start = 0
        for f, width in enumerate(chan_splits):
            pieces = exchange(mixes[f * parts : (f + 1) * parts], "ctx", parts)
            backed = outer(pieces, kern, fwd, back, turn, sizes, start, backed)
            start += width

        up_one, up_two, down_one, down_two = expand_factors(
            right_up, left_up, right_down, left_down, me, groups
        )
        last = xor_blocks(inv_inner, 1, at, parts)
        out = None
        row = 0
        for j, size in enumerate(sizes):
            home = exchange(backed[j * parts : (j + 1) * parts], "ctx", parts)
            mixed, *pieces = mix(home, tok, scale, gain, gain_two, last, up_one, row, groups)
            pieces = exchange(pieces, "hid", groups)
            pieces = hidden(pieces, up_two, down_one, total)
            pieces = exchange(pieces, "hid", groups)
            out = final(pieces, mixed, down_two, row * block, count, out)
            row += size
        return out.reshape(1, count, chans)

    return shards


def solution(mesh):
    return jax.shard_map(
        make_shards(mesh.shape["ctx"], mesh.shape["hid"]),
        mesh=mesh,
        in_specs=(
            P(None, "ctx", "hid"),
            P(),
            P(),
            P(),
            P(),
            P("ctx", None),
            P(None, "ctx"),
            P("ctx", None, "hid"),
            P("hid"),
            P("hid"),
            P("hid", None, None),
            P("hid", None, None),
            P("hid", None, None),
            P("hid", None, None),
        ),
        out_specs=P(None, "ctx", "hid"),
        check_vma=False,
    )
```

```python
import math

import jax
import jax.numpy as jnp
from jax import lax
from jax.experimental import pallas as pl
from jax.experimental.pallas import tpu as pltpu
from jax.sharding import PartitionSpec as P

EPS = 1e-06
G = 16
ROWS = 256
TAIL = 16
LANES = 128
BF = jnp.bfloat16
F32 = jnp.float32

RETURN_SPLIT = (2, 4, 4, 4, 2)


def cost(flops, moved, exps=0):
    return pl.CostEstimate(flops=int(flops), bytes_accessed=int(moved), transcendentals=int(exps))


def dot(a, b):
    return jnp.dot(a, b, preferred_element_type=F32)


def whole(shape):
    zeros = (0,) * len(shape)
    return pl.BlockSpec(shape, lambda *_: zeros, pipeline_mode=pl.Buffered(1))


def xor_blocks(x, axis, me, parts):
    size = x.shape[axis] // parts
    return jnp.concatenate(
        [lax.dynamic_slice_in_dim(x, (me ^ d) * size, size, axis) for d in range(parts)], axis
    )


def after(x, *needed):
    return lax.optimization_barrier((x, needed))[0]


def swap(x, name, size, d):
    return lax.ppermute(x, name, [(i, i ^ d) for i in range(size)])


def exchange(pieces, name, size):
    order = sorted(range(1, size), key=lambda d: -d)
    got = {d: swap(pieces[d], name, size, d) for d in order}
    return [pieces[0]] + [got[d] for d in range(1, size)]


def inner_kernel(parts, tok, scale, gain, mix, twiddle, *refs):
    outs, rows_of = refs[:parts], refs[parts]
    block = mix.shape[0]
    al = tok.shape[0] // block
    ql = block // parts
    for a in range(al):
        at = pl.ds(a * block, block)
        normed = (tok[at, :].astype(F32) * (gain[...] * scale[at, :])).astype(BF)
        rows_of[at, :] = dot(mix[...], normed) * twiddle[a]
    for d in range(parts):
        for q in range(ql):
            outs[d][q] = rows_of[pl.ds(d * ql + q, al, stride=block), :].astype(BF)


def inner(tokens, scale, gain, mix, twiddle, parts):
    count, chans = tokens.shape
    block = mix.shape[0]
    al = count // block
    ql = block // parts
    cb = LANES
    return pl.pallas_call(
        lambda *refs: inner_kernel(parts, *refs),
        grid=(chans // cb,),
        in_specs=[
            pl.BlockSpec((count, cb), lambda c: (0, c)),
            whole((count, 1)),
            pl.BlockSpec((1, cb), lambda c: (0, c)),
            whole((block, block)),
            whole((al, block, 1)),
        ],
        out_specs=[pl.BlockSpec((ql, al, cb), lambda c: (0, 0, c)) for _ in range(parts)],
        out_shape=[jax.ShapeDtypeStruct((ql, al, chans), BF) for _ in range(parts)],
        scratch_shapes=[pltpu.VMEM((count, cb), F32)],
        cost_estimate=cost(2 * count * block * chans, 4 * count * chans),
        name="inner_mix",
    )(tokens, scale, gain, mix, twiddle)


def outer_kernel(parts, sizes, *refs):
    pieces = refs[:parts]
    kern, fwd, back, twiddle = refs[parts : parts + 4]
    outs, rows_of = refs[parts + 4 : -1], refs[-1]
    width = kern.shape[-1]
    side = twiddle.shape[1]
    pair = fwd.shape[0] // side
    al = side // parts
    for q in range(0, G, pair):
        x = jnp.concatenate([p[q + i] for i in range(pair) for p in pieces], axis=0)
        k = jnp.concatenate([kern[:, q + i].reshape(side, width) for i in range(pair)], axis=0)
        mixed = dot(fwd[...], x).astype(BF)
        filtered = (mixed.astype(F32) * k.astype(F32)).astype(BF)
        backed = dot(back[...], filtered)
        for i in range(pair):
            turned = backed[i * side : (i + 1) * side] * twiddle[q + i]
            for c in range(width // LANES):
                rows_of[c, pl.ds((q + i) * side, side), :] = turned[:, c * LANES : (c + 1) * LANES]
    for d in range(parts):
        r = d * al
        for out, size in zip(outs, sizes, strict=True):
            for i in range(size):
                for c in range(width // LANES):
                    out[d, i, :, c * LANES : (c + 1) * LANES] = rows_of[
                        c, pl.ds(r, G, stride=side), :
                    ].astype(BF)
                r += 1


def outer(pieces, kern, fwd, back, twiddle, sizes):
    parts = len(pieces)
    ql, al, chans = pieces[0].shape
    side = parts * al
    cb = 256
    return pl.pallas_call(
        lambda *refs: outer_kernel(parts, sizes, *refs),
        grid=(chans // cb, ql // G),
        in_specs=[pl.BlockSpec((G, al, cb), lambda c, q: (q, 0, c)) for _ in range(parts)]
        + [
            pl.BlockSpec((parts, G, al, cb), lambda c, q: (0, q, 0, c)),
            whole(fwd.shape),
            whole(back.shape),
            pl.BlockSpec((G, side, 1), lambda c, q: (q, 0, 0)),
        ],
        out_specs=[pl.BlockSpec((parts, size, G, cb), lambda c, q: (0, 0, q, c)) for size in sizes],
        out_shape=[jax.ShapeDtypeStruct((parts, size, ql, chans), BF) for size in sizes],
        scratch_shapes=[pltpu.VMEM((cb // LANES, G * side, LANES), F32)],
        cost_estimate=cost(8 * side * side * ql * chans, 6 * side * ql * chans),
        name="outer_mix",
    )(*pieces, kern, fwd, back, twiddle)


def eye_at(rows, cols, first):
    return iota((rows, cols), 0) == iota((rows, cols), 1) + first


def mix_kernel(groups, pieces, tok, scale, gain, gain_two, back, up, mixed_out, *outs):
    block, chans = tok.shape
    conv = dot(back[...], pieces[...].reshape(block, chans))
    wide = tok[...].astype(F32)
    normed = (wide * (gain[...] * scale[...])).astype(BF).astype(F32)
    mixed = wide + conv * (normed / (1.0 + jnp.exp(-normed)))
    mixed_out[...] = mixed
    projected = dot((mixed * gain_two[...]).astype(BF), up[...]).astype(BF)
    width = projected.shape[1] // groups
    sums = jnp.sum(mixed * mixed, axis=1, keepdims=True)
    tail = jnp.zeros((TAIL, width), F32)
    line = iota((TAIL, width), 0)
    for u in range(block // width):
        row = jnp.sum(jnp.where(eye_at(block, width, u * width), sums, 0.0), axis=0, keepdims=True)
        for part in range(3):
            piece = row.astype(BF).astype(F32)
            tail = jnp.where(line == 3 * u + part, piece, tail)
            row = row - piece
    for d in range(groups):
        outs[d][0, :block] = projected[:, d * width : (d + 1) * width]
        outs[d][0, block:] = tail.astype(BF)


def mix(home, tokens, scale, gain, gain_two, back, up, row, groups):
    parts, size, ql, chans = home.shape
    block = ql * parts
    count = size * block
    width = up.shape[1] // groups
    return pl.pallas_call(
        lambda *refs: mix_kernel(groups, *refs),
        grid=(size,),
        in_specs=[
            pl.BlockSpec((parts, 1, ql, chans), lambda r: (0, r, 0, 0)),
            pl.BlockSpec((block, chans), lambda r: (r + row, 0)),
            pl.BlockSpec((block, 1), lambda r: (r + row, 0)),
            whole((1, chans)),
            whole((1, chans)),
            whole((block, block)),
            whole(up.shape),
        ],
        out_specs=[pl.BlockSpec((block, chans), lambda r: (r, 0))]
        + [pl.BlockSpec((1, block + TAIL, width), lambda r: (r, 0, 0)) for _ in range(groups)],
        out_shape=[jax.ShapeDtypeStruct((count, chans), F32)]
        + [jax.ShapeDtypeStruct((size, block + TAIL, width), BF) for _ in range(groups)],
        cost_estimate=cost(2 * count * chans * (block + up.shape[1]), 10 * count * chans, count * chans),
        name="mix_tokens",
    )(home, tokens, scale, gain, gain_two, back, up)


def hidden_kernel(groups, total, halves, *refs):
    pieces = refs[:groups]
    up, down = refs[groups : groups + 2]
    outs = refs[groups + 2 :]
    width = pieces[0].shape[2]
    block = pieces[0].shape[1] - TAIL
    tail = sum(p[0, block:].astype(F32) for p in pieces)
    sums = jnp.zeros((block, 1), F32)
    for u in range(block // width):
        row = tail[3 * u : 3 * u + 1] + tail[3 * u + 1 : 3 * u + 2] + tail[3 * u + 2 : 3 * u + 3]
        sums = sums + jnp.sum(jnp.where(eye_at(block, width, u * width), row, 0.0), axis=1, keepdims=True)
    scale = lax.rsqrt(sums / total + EPS)
    part = width // halves
    inside, middle = up.shape[0] // halves, up.shape[1] // halves
    outside = down.shape[1] // halves
    step = outside // groups
    for h in range(halves):
        x = jnp.concatenate([p[0, :block, h * part : (h + 1) * part] for p in pieces], axis=1)
        up_h = up[h * inside : (h + 1) * inside, h * middle : (h + 1) * middle]
        down_h = down[h * middle : (h + 1) * middle, h * outside : (h + 1) * outside]
        v = dot(x, up_h) * scale
        active = (0.5 * v * (1.0 + jnp.tanh(0.7978845608 * (v + 0.044715 * (v * v * v))))).astype(BF)
        reduced = dot(active, down_h).astype(BF)
        for d in range(groups):
            outs[d][:, h * step : (h + 1) * step] = reduced[:, d * step : (d + 1) * step]


def hidden(pieces, up, down, total, halves):
    groups = len(pieces)
    size, tall, width = pieces[0].shape
    block = tall - TAIL
    count = size * block
    step = down.shape[1] // groups
    return pl.pallas_call(
        lambda *refs: hidden_kernel(groups, total, halves, *refs),
        grid=(size,),
        in_specs=[pl.BlockSpec((1, tall, width), lambda t: (t, 0, 0)) for _ in range(groups)]
        + [whole(up.shape), whole(down.shape)],
        out_specs=[pl.BlockSpec((block, step), lambda t: (t, 0)) for _ in range(groups)],
        out_shape=[jax.ShapeDtypeStruct((count, step), BF) for _ in range(groups)],
        cost_estimate=cost(
            2 * count * up.shape[1] * (up.shape[0] + down.shape[1]) // halves,
            2 * groups * count * (width + step),
            count * up.shape[1],
        ),
        name="hidden_units",
    )(*pieces, up, down)


def final_kernel(groups, *refs):
    pieces = refs[:groups]
    mixed, left = refs[groups : groups + 2]
    out = refs[-1]
    x = jnp.concatenate([p[...] for p in pieces], axis=1)
    out[...] = (mixed[...] + dot(x, left[...])).astype(BF)


def final(pieces, mixed, left, row, count_all, carried):
    groups = len(pieces)
    count, step = pieces[0].shape
    chans = mixed.shape[1]
    tb = min(ROWS, count)
    first = row // tb
    extra = [] if carried is None else [carried]
    return pl.pallas_call(
        lambda *refs: final_kernel(groups, *refs),
        grid=(count // tb,),
        in_specs=[pl.BlockSpec((tb, step), lambda t: (t, 0)) for _ in range(groups)]
        + [pl.BlockSpec((tb, chans), lambda t: (t, 0)), whole(left.shape)]
        + [pl.BlockSpec(memory_space=pl.ANY) for _ in extra],
        out_specs=pl.BlockSpec((tb, chans), lambda t: (t + first, 0)),
        out_shape=jax.ShapeDtypeStruct((count_all, chans), BF),
        input_output_aliases={groups + 2: 0} if extra else {},
        cost_estimate=cost(2 * count * groups * step * chans, 8 * count * chans),
        name="block_out",
    )(*pieces, mixed, left, *extra)


def iota(shape, axis):
    return lax.broadcasted_iota(jnp.int32, shape, axis)


def pick(rows, cols, of_col):
    return (iota((rows, cols), 0) == of_col(iota((rows, cols), 1))).astype(BF)


def masked(x, keep):
    rows, cols = iota(x.shape, 0), iota(x.shape, 1)
    return jnp.where(keep(rows, cols), x, 0.0).astype(BF)


def repeat_block(x, times):
    rows, cols = x.shape
    return masked(
        jnp.tile(x.astype(F32), (times, times)), lambda r, c: r // rows == c // cols
    )


def expand_factors(right_up, left_up, right_down, left_down, me, groups, halves):
    il, nj, nk = right_up.shape
    kl, ni, nm = left_up.shape
    nq = right_down.shape[2]
    ql, nkk, nr = left_down.shape
    lk, lr = kl * il, ql * kl

    def place(at, lanes):
        part = lanes // halves
        half, rest = at // (groups * part), at % (groups * part)
        return rest // part, half * part + rest % part

    def up_two_source(r):
        d, lane = place(r, lk)
        return (lane // il) * ni + (me ^ d) * il + lane % il

    def down_one_source(c):
        d, lane = place(c, lr)
        return (me ^ d) * ql + lane % ql

    def down_two_source(r):
        lane = r % lr
        return (lane % ql) * nkk + (me ^ (r // lr)) * kl + lane // ql

    up_one = masked(
        dot(
            right_up.reshape(il * nj, nk),
            pick(nk, groups * lk, lambda c: (me ^ (c // lk)) * kl + c % lk // il),
        ),
        lambda r, c: r // nj == c % il,
    )
    rows = groups * lk
    taken = dot(pick(kl * ni, rows, up_two_source).T, left_up.reshape(kl * ni, nm))
    up_two = masked(
        jnp.tile(taken, (1, kl)), lambda r, c: c // nm == place(r, lk)[1] // il
    )
    down_one = masked(
        dot(right_down.reshape(kl * nm, nq), pick(nq, groups * lr, down_one_source)),
        lambda r, c: r // nm == place(c, lr)[1] // ql,
    )
    rows = groups * lr
    taken = dot(pick(ql * nkk, rows, down_two_source).T, left_down.reshape(ql * nkk, nr)).astype(BF)
    down_two = masked(
        dot(taken, pick(nr, ql * nr, lambda c: c % nr)),
        lambda r, c: c // nr == r % lr % ql,
    )
    return up_one, up_two, down_one, down_two


def splits_of(total, shares):
    unit = total // sum(shares)
    if unit * sum(shares) != total:
        return [total]
    return [unit * share for share in shares]


def make_shards(parts, groups):
    def shards(
        tokens,
        seq_inner,
        seq_outer,
        inv_outer,
        inv_inner,
        twiddle_in,
        twiddle_out,
        freq_kernel,
        first_gain,
        second_gain,
        right_up,
        left_up,
        right_down,
        left_down,
    ):
        _, count, chans = tokens.shape
        total = chans * groups
        block = seq_inner.shape[0]
        ql = block // parts
        al = count // block
        at = lax.axis_index("ctx")
        me = lax.axis_index("hid")
        tok = tokens.reshape(count, chans)

        sent = freq_kernel.reshape(al, parts, ql, chans).transpose(1, 2, 0, 3)
        kern = lax.all_to_all(sent, "ctx", split_axis=0, concat_axis=0, tiled=True)

        wide = tok.astype(F32)
        sums = lax.psum(jnp.sum(wide * wide, axis=1), "hid")
        scale = lax.rsqrt(sums / total + EPS).reshape(count, 1)
        gain = first_gain.reshape(1, chans)
        gain_two = second_gain.reshape(1, chans)

        pieces = inner(
            tok,
            scale,
            gain,
            xor_blocks(seq_inner, 0, at, parts),
            xor_blocks(twiddle_in, 1, at, parts).reshape(al, block, 1),
            parts,
        )
        fwd = repeat_block(xor_blocks(seq_outer, 1, at, parts), 2)
        back = repeat_block(inv_outer, 2)
        turn = twiddle_out.T.reshape(ql, al * parts, 1)
        sizes = splits_of(al, RETURN_SPLIT)
        pieces = exchange(pieces, "ctx", parts)

        lanes = right_up.shape[0] * left_up.shape[0]
        halves = lanes // 128 if lanes % 128 == 0 else 1
        up_one, up_two, down_one, down_two = expand_factors(
            right_up, left_up, right_down, left_down, me, groups, halves
        )
        kern = after(kern, up_one, up_two, down_one, down_two, turn)
        backed = outer(pieces, kern, fwd, back, turn, sizes)
        chunks = len(sizes)
        starts = [sum(sizes[:j]) for j in range(chunks)]
        mixed, ups, downs, done = {}, {}, {}, {}
        out = None

        def hide(j):
            downs[j] = hidden(ups[j], up_two, down_one, total, halves)
            done[j] = downs[j][0]
            downs[j] = exchange(downs[j], "hid", groups)

        def finish(j, out):
            return final(downs[j], mixed[j], down_two, starts[j] * block, count, out)

        for j in range(chunks):
            needed = []
            if j >= 2:
                needed.append(mixed[j - 2])
            if j >= 3:
                needed.append(done[j - 3])
            if j >= 4:
                needed.append(out)
            sent = after(backed[j], *needed) if needed else backed[j]
            home = lax.all_to_all(sent, "ctx", split_axis=0, concat_axis=0, tiled=True)
            mixed[j], *pieces = mix(
                home, tok, scale, gain, gain_two, inv_inner, up_one, starts[j], groups
            )
            ups[j] = exchange(pieces, "hid", groups)
            if j >= 1:
                hide(j - 1)
            if j >= 2:
                out = finish(j - 2, out)
        hide(chunks - 1)
        for j in range(max(chunks - 2, 0), chunks):
            out = finish(j, out)
        return out.reshape(1, count, chans)

    return shards


def solution(mesh):
    return jax.shard_map(
        make_shards(mesh.shape["ctx"], mesh.shape["hid"]),
        mesh=mesh,
        in_specs=(
            P(None, "ctx", "hid"),
            P(),
            P(),
            P(),
            P(),
            P("ctx", None),
            P(None, "ctx"),
            P("ctx", None, "hid"),
            P("hid"),
            P("hid"),
            P("hid", None, None),
            P("hid", None, None),
            P("hid", None, None),
            P("hid", None, None),
        ),
        out_specs=P(None, "ctx", "hid"),
        check_vma=False,
    )
```

```python
import math

import jax
import jax.numpy as jnp
from jax import lax
from jax.experimental import pallas as pl
from jax.experimental.pallas import tpu as pltpu
from jax.sharding import PartitionSpec as P

EPS = 1e-06
G = 16
ROWS = 256
TAIL = 16
LANES = 128
BF = jnp.bfloat16
F32 = jnp.float32

RETURN_SPLIT = (4, 4, 5, 3)


def cost(flops, moved, exps=0):
    return pl.CostEstimate(flops=int(flops), bytes_accessed=int(moved), transcendentals=int(exps))


def dot(a, b):
    return jnp.dot(a, b, preferred_element_type=F32)


def whole(shape):
    zeros = (0,) * len(shape)
    return pl.BlockSpec(shape, lambda *_: zeros, pipeline_mode=pl.Buffered(1))


def xor_blocks(x, axis, me, parts):
    size = x.shape[axis] // parts
    return jnp.concatenate(
        [lax.dynamic_slice_in_dim(x, (me ^ d) * size, size, axis) for d in range(parts)], axis
    )


def after(x, *needed):
    return lax.optimization_barrier((x, needed))[0]


def swap(x, name, size, d):
    return lax.ppermute(x, name, [(i, i ^ d) for i in range(size)])


def exchange(pieces, name, size):
    if len(pieces) != size:
        return [lax.all_to_all(pieces[0], name, split_axis=0, concat_axis=0, tiled=True)]
    order = sorted(range(1, size), key=lambda d: -d)
    got = {d: swap(pieces[d], name, size, d) for d in order}
    return [pieces[0]] + [got[d] for d in range(1, size)]


def inner_kernel(parts, tok, scale, gain, mix, twiddle, *refs):
    outs, rows_of = refs[:parts], refs[parts]
    block = mix.shape[0]
    al = tok.shape[0] // block
    ql = block // parts
    for a in range(al):
        at = pl.ds(a * block, block)
        normed = (tok[at, :].astype(F32) * (gain[...] * scale[at, :])).astype(BF)
        rows_of[at, :] = dot(mix[...], normed) * twiddle[a]
    for d in range(parts):
        for q in range(ql):
            outs[d][q] = rows_of[pl.ds(d * ql + q, al, stride=block), :].astype(BF)


def inner(tokens, scale, gain, mix, twiddle, parts):
    count, chans = tokens.shape
    block = mix.shape[0]
    al = count // block
    ql = block // parts
    cb = LANES
    return pl.pallas_call(
        lambda *refs: inner_kernel(parts, *refs),
        grid=(chans // cb,),
        in_specs=[
            pl.BlockSpec((count, cb), lambda c: (0, c)),
            whole((count, 1)),
            pl.BlockSpec((1, cb), lambda c: (0, c)),
            whole((block, block)),
            whole((al, block, 1)),
        ],
        out_specs=[pl.BlockSpec((ql, al, cb), lambda c: (0, 0, c)) for _ in range(parts)],
        out_shape=[jax.ShapeDtypeStruct((ql, al, chans), BF) for _ in range(parts)],
        scratch_shapes=[pltpu.VMEM((count, cb), F32)],
        cost_estimate=cost(2 * count * block * chans, 4 * count * chans),
        name="inner_mix",
    )(tokens, scale, gain, mix, twiddle)


def outer_kernel(parts, sizes, *refs):
    pieces = refs[:parts]
    kern, fwd, back, twiddle = refs[parts : parts + 4]
    outs, rows_of = refs[parts + 4 : -1], refs[-1]
    width = kern.shape[-1]
    side = twiddle.shape[1]
    pair = fwd.shape[0] // side
    al = side // parts
    for q in range(0, G, pair):
        x = jnp.concatenate([p[q + i] for i in range(pair) for p in pieces], axis=0)
        k = jnp.concatenate([kern[:, q + i].reshape(side, width) for i in range(pair)], axis=0)
        mixed = dot(fwd[...], x).astype(BF)
        filtered = (mixed.astype(F32) * k.astype(F32)).astype(BF)
        backed = dot(back[...], filtered)
        for i in range(pair):
            turned = backed[i * side : (i + 1) * side] * twiddle[q + i]
            for c in range(width // LANES):
                rows_of[c, pl.ds((q + i) * side, side), :] = turned[:, c * LANES : (c + 1) * LANES]
    for d in range(parts):
        r = d * al
        for out, size in zip(outs, sizes, strict=True):
            for i in range(size):
                for c in range(width // LANES):
                    out[d, i, :, c * LANES : (c + 1) * LANES] = rows_of[
                        c, pl.ds(r, G, stride=side), :
                    ].astype(BF)
                r += 1


def outer(pieces, kern, fwd, back, twiddle, sizes):
    parts = len(pieces)
    ql, al, chans = pieces[0].shape
    side = parts * al
    cb = 256
    return pl.pallas_call(
        lambda *refs: outer_kernel(parts, sizes, *refs),
        grid=(chans // cb, ql // G),
        in_specs=[pl.BlockSpec((G, al, cb), lambda c, q: (q, 0, c)) for _ in range(parts)]
        + [
            pl.BlockSpec((parts, G, al, cb), lambda c, q: (0, q, 0, c)),
            whole(fwd.shape),
            whole(back.shape),
            pl.BlockSpec((G, side, 1), lambda c, q: (q, 0, 0)),
        ],
        out_specs=[pl.BlockSpec((parts, size, G, cb), lambda c, q: (0, 0, q, c)) for size in sizes],
        out_shape=[jax.ShapeDtypeStruct((parts, size, ql, chans), BF) for size in sizes],
        scratch_shapes=[pltpu.VMEM((cb // LANES, G * side, LANES), F32)],
        cost_estimate=cost(8 * side * side * ql * chans, 6 * side * ql * chans),
        name="outer_mix",
    )(*pieces, kern, fwd, back, twiddle)


def eye_at(rows, cols, first):
    return iota((rows, cols), 0) == iota((rows, cols), 1) + first


def places(refs, groups, me):
    return refs if len(refs) == groups else [refs[0].at[me[0] ^ d] for d in range(groups)]


def mix_kernel(groups, me, pieces, tok, scale, gain, gain_two, back, up, mixed_out, *outs):
    outs = places(outs, groups, me)
    block, chans = tok.shape
    conv = dot(back[...], pieces[...].reshape(block, chans))
    wide = tok[...].astype(F32)
    normed = (wide * (gain[...] * scale[...])).astype(BF).astype(F32)
    mixed = wide + conv * (normed / (1.0 + jnp.exp(-normed)))
    mixed_out[...] = mixed
    projected = dot((mixed * gain_two[...]).astype(BF), up[...]).astype(BF)
    width = projected.shape[1] // groups
    sums = jnp.sum(mixed * mixed, axis=1, keepdims=True)
    tail = jnp.zeros((TAIL, width), F32)
    line = iota((TAIL, width), 0)
    for u in range(block // width):
        row = jnp.sum(jnp.where(eye_at(block, width, u * width), sums, 0.0), axis=0, keepdims=True)
        for part in range(3):
            piece = row.astype(BF).astype(F32)
            tail = jnp.where(line == 3 * u + part, piece, tail)
            row = row - piece
    for d in range(groups):
        outs[d][0, :block] = projected[:, d * width : (d + 1) * width]
        outs[d][0, block:] = tail.astype(BF)


def fan(shape, index, groups, stacked):
    if stacked:
        return [pl.BlockSpec((groups,) + shape, lambda t: (0,) + index(t))]
    return [pl.BlockSpec(shape, index) for _ in range(groups)]


def fan_out(shape, groups, stacked):
    if stacked:
        return [jax.ShapeDtypeStruct((groups,) + shape, BF)]
    return [jax.ShapeDtypeStruct(shape, BF) for _ in range(groups)]


SCALAR = pl.BlockSpec(memory_space=pltpu.SMEM)


def mix(me, home, tokens, scale, gain, gain_two, back, up, row, groups, stacked):
    parts, size, ql, chans = home.shape
    block = ql * parts
    count = size * block
    width = up.shape[1] // groups
    return pl.pallas_call(
        lambda *refs: mix_kernel(groups, *refs),
        grid=(size,),
        in_specs=[
            SCALAR,
            pl.BlockSpec((parts, 1, ql, chans), lambda r: (0, r, 0, 0)),
            pl.BlockSpec((block, chans), lambda r: (r + row, 0)),
            pl.BlockSpec((block, 1), lambda r: (r + row, 0)),
            whole((1, chans)),
            whole((1, chans)),
            whole((block, block)),
            whole(up.shape),
        ],
        out_specs=[pl.BlockSpec((block, chans), lambda r: (r, 0))]
        + fan((1, block + TAIL, width), lambda r: (r, 0, 0), groups, stacked),
        out_shape=[jax.ShapeDtypeStruct((count, chans), F32)]
        + fan_out((size, block + TAIL, width), groups, stacked),
        cost_estimate=cost(2 * count * chans * (block + up.shape[1]), 10 * count * chans, count * chans),
        name="mix_tokens",
    )(me, home, tokens, scale, gain, gain_two, back, up)


def hidden_kernel(groups, total, halves, me, up, down, *refs):
    pieces = places(refs[: len(refs) // 2], groups, me)
    outs = places(refs[len(refs) // 2 :], groups, me)
    width = pieces[0].shape[2]
    block = pieces[0].shape[1] - TAIL
    tail = sum(p[0, block:].astype(F32) for p in pieces)
    sums = jnp.zeros((block, 1), F32)
    for u in range(block // width):
        row = tail[3 * u : 3 * u + 1] + tail[3 * u + 1 : 3 * u + 2] + tail[3 * u + 2 : 3 * u + 3]
        sums = sums + jnp.sum(jnp.where(eye_at(block, width, u * width), row, 0.0), axis=1, keepdims=True)
    scale = lax.rsqrt(sums / total + EPS)
    part = width // halves
    inside, middle = up.shape[0] // halves, up.shape[1] // halves
    outside = down.shape[1] // halves
    step = outside // groups
    for h in range(halves):
        x = jnp.concatenate([p[0, :block, h * part : (h + 1) * part] for p in pieces], axis=1)
        up_h = up[h * inside : (h + 1) * inside, h * middle : (h + 1) * middle]
        down_h = down[h * middle : (h + 1) * middle, h * outside : (h + 1) * outside]
        v = dot(x, up_h) * scale
        active = (0.5 * v * (1.0 + jnp.tanh(0.7978845608 * (v + 0.044715 * (v * v * v))))).astype(BF)
        reduced = dot(active, down_h).astype(BF)
        for d in range(groups):
            outs[d][:, h * step : (h + 1) * step] = reduced[:, d * step : (d + 1) * step]


def hidden(me, pieces, up, down, total, halves, groups):
    stacked = len(pieces) != groups
    size, tall, width = pieces[0].shape[-3:]
    block = tall - TAIL
    count = size * block
    step = down.shape[1] // groups
    return pl.pallas_call(
        lambda *refs: hidden_kernel(groups, total, halves, *refs),
        grid=(size,),
        in_specs=[SCALAR, whole(up.shape), whole(down.shape)]
        + fan((1, tall, width), lambda t: (t, 0, 0), groups, stacked),
        out_specs=fan((block, step), lambda t: (t, 0), groups, stacked),
        out_shape=fan_out((count, step), groups, stacked),
        cost_estimate=cost(
            2 * count * up.shape[1] * (up.shape[0] + down.shape[1]) // halves,
            2 * groups * count * (width + step),
            count * up.shape[1],
        ),
        name="hidden_units",
    )(me, up, down, *pieces)


def final_kernel(groups, me, mixed, left, *refs):
    pieces = places(refs[: 1 if len(refs) < groups else groups], groups, me)
    out = refs[-1]
    x = jnp.concatenate([p[...] for p in pieces], axis=1)
    out[...] = (mixed[...] + dot(x, left[...])).astype(BF)


def final(me, pieces, mixed, left, row, count_all, carried, groups):
    stacked = len(pieces) != groups
    count, step = pieces[0].shape[-2:]
    chans = mixed.shape[1]
    tb = min(ROWS, count)
    first = row // tb
    extra = [] if carried is None else [carried]
    return pl.pallas_call(
        lambda *refs: final_kernel(groups, *refs),
        grid=(count // tb,),
        in_specs=[SCALAR, pl.BlockSpec((tb, chans), lambda t: (t, 0)), whole(left.shape)]
        + fan((tb, step), lambda t: (t, 0), groups, stacked)
        + [pl.BlockSpec(memory_space=pl.ANY) for _ in extra],
        out_specs=pl.BlockSpec((tb, chans), lambda t: (t + first, 0)),
        out_shape=jax.ShapeDtypeStruct((count_all, chans), BF),
        input_output_aliases={3 + len(pieces): 0} if extra else {},
        cost_estimate=cost(2 * count * groups * step * chans, 8 * count * chans),
        name="block_out",
    )(me, mixed, left, *pieces, *extra)


def iota(shape, axis):
    return lax.broadcasted_iota(jnp.int32, shape, axis)


def pick(rows, cols, of_col):
    return (iota((rows, cols), 0) == of_col(iota((rows, cols), 1))).astype(BF)


def masked(x, keep):
    rows, cols = iota(x.shape, 0), iota(x.shape, 1)
    return jnp.where(keep(rows, cols), x, 0.0).astype(BF)


def repeat_block(x, times):
    rows, cols = x.shape
    return masked(
        jnp.tile(x.astype(F32), (times, times)), lambda r, c: r // rows == c // cols
    )


def expand_factors(right_up, left_up, right_down, left_down, me, groups, halves):
    il, nj, nk = right_up.shape
    kl, ni, nm = left_up.shape
    nq = right_down.shape[2]
    ql, nkk, nr = left_down.shape
    lk, lr = kl * il, ql * kl

    def place(at, lanes):
        part = lanes // halves
        half, rest = at // (groups * part), at % (groups * part)
        return rest // part, half * part + rest % part

    def up_two_source(r):
        d, lane = place(r, lk)
        return (lane // il) * ni + (me ^ d) * il + lane % il

    def down_one_source(c):
        d, lane = place(c, lr)
        return (me ^ d) * ql + lane % ql

    def down_two_source(r):
        lane = r % lr
        return (lane % ql) * nkk + (me ^ (r // lr)) * kl + lane // ql

    up_one = masked(
        dot(
            right_up.reshape(il * nj, nk),
            pick(nk, groups * lk, lambda c: (me ^ (c // lk)) * kl + c % lk // il),
        ),
        lambda r, c: r // nj == c % il,
    )
    rows = groups * lk
    taken = dot(pick(kl * ni, rows, up_two_source).T, left_up.reshape(kl * ni, nm))
    up_two = masked(
        jnp.tile(taken, (1, kl)), lambda r, c: c // nm == place(r, lk)[1] // il
    )
    down_one = masked(
        dot(right_down.reshape(kl * nm, nq), pick(nq, groups * lr, down_one_source)),
        lambda r, c: r // nm == place(c, lr)[1] // ql,
    )
    rows = groups * lr
    taken = dot(pick(ql * nkk, rows, down_two_source).T, left_down.reshape(ql * nkk, nr)).astype(BF)
    down_two = masked(
        dot(taken, pick(nr, ql * nr, lambda c: c % nr)),
        lambda r, c: c // nr == r % lr % ql,
    )
    return up_one, up_two, down_one, down_two


def splits_of(total, shares):
    unit = total // sum(shares)
    if unit * sum(shares) != total:
        return [total]
    return [unit * share for share in shares]


def make_shards(parts, groups):
    def shards(
        tokens,
        seq_inner,
        seq_outer,
        inv_outer,
        inv_inner,
        twiddle_in,
        twiddle_out,
        freq_kernel,
        first_gain,
        second_gain,
        right_up,
        left_up,
        right_down,
        left_down,
    ):
        _, count, chans = tokens.shape
        total = chans * groups
        block = seq_inner.shape[0]
        ql = block // parts
        al = count // block
        at = lax.axis_index("ctx")
        me = lax.axis_index("hid")
        tok = tokens.reshape(count, chans)

        sent = freq_kernel.reshape(al, parts, ql, chans).transpose(1, 2, 0, 3)
        kern = lax.all_to_all(sent, "ctx", split_axis=0, concat_axis=0, tiled=True)

        wide = tok.astype(F32)
        sums = lax.psum(jnp.sum(wide * wide, axis=1), "hid")
        scale = lax.rsqrt(sums / total + EPS).reshape(count, 1)
        gain = first_gain.reshape(1, chans)
        gain_two = second_gain.reshape(1, chans)

        pieces = inner(
            tok,
            scale,
            gain,
            xor_blocks(seq_inner, 0, at, parts),
            xor_blocks(twiddle_in, 1, at, parts).reshape(al, block, 1),
            parts,
        )
        fwd = repeat_block(xor_blocks(seq_outer, 1, at, parts), 2)
        back = repeat_block(inv_outer, 2)
        turn = twiddle_out.T.reshape(ql, al * parts, 1)
        sizes = splits_of(al, RETURN_SPLIT)
        pieces = exchange(pieces, "ctx", parts)

        lanes = right_up.shape[0] * left_up.shape[0]
        halves = lanes // 128 if lanes % 128 == 0 else 1
        up_one, up_two, down_one, down_two = expand_factors(
            right_up, left_up, right_down, left_down, me, groups, halves
        )
        kern = after(kern, up_one, up_two, down_one, down_two, turn)
        backed = outer(pieces, kern, fwd, back, turn, sizes)
        chunks = len(sizes)
        place = me.astype(jnp.int32).reshape(1)
        starts = [sum(sizes[:j]) for j in range(chunks)]
        mixed, ups, downs, done, outs = {}, {}, {}, {}, {-1: None}

        def hide(j):
            pieces = ups[j]
            if 1 <= j < chunks - 1:
                pieces = after(pieces, mixed[j + 1])
            if j >= 1:
                pieces = after(pieces, downs[j - 1])
            pieces = hidden(place, pieces, up_two, down_one, total, halves, groups)
            done[j] = pieces
            downs[j] = exchange(pieces, "hid", groups)

        def finish(j):
            outs[j] = final(
                place, downs[j], mixed[j], down_two, starts[j] * block, count, outs[j - 1], groups
            )

        for j in range(chunks):
            needed = []
            if j >= 2:
                needed.append(ups[j - 2])
            if j >= 3:
                needed.append(done[j - 3])
            if j >= 4:
                needed.append(outs[j - 4])
            sent = after(backed[j], *needed) if needed else backed[j]
            home = lax.all_to_all(sent, "ctx", split_axis=0, concat_axis=0, tiled=True)
            mixed[j], *pieces = mix(
                place,
                home,
                tok,
                scale,
                gain,
                gain_two,
                inv_inner,
                up_one,
                starts[j],
                groups,
                j == chunks - 1,
            )
            ups[j] = exchange(pieces, "hid", groups)
            if j >= 1:
                hide(j - 1)
            if j >= 2:
                finish(j - 2)
        hide(chunks - 1)
        for j in range(max(chunks - 2, 0), chunks):
            finish(j)
        return outs[chunks - 1].reshape(1, count, chans)

    return shards


def solution(mesh):
    return jax.shard_map(
        make_shards(mesh.shape["ctx"], mesh.shape["hid"]),
        mesh=mesh,
        in_specs=(
            P(None, "ctx", "hid"),
            P(),
            P(),
            P(),
            P(),
            P("ctx", None),
            P(None, "ctx"),
            P("ctx", None, "hid"),
            P("hid"),
            P("hid"),
            P("hid", None, None),
            P("hid", None, None),
            P("hid", None, None),
            P("hid", None, None),
        ),
        out_specs=P(None, "ctx", "hid"),
        check_vma=False,
    )
```

```python
import math

import jax
import jax.numpy as jnp
from jax import lax
from jax.experimental import pallas as pl
from jax.experimental.pallas import tpu as pltpu
from jax.sharding import PartitionSpec as P

EPS = 1e-06
G = 16
ROWS = 256
TAIL = 16
LANES = 128
BF = jnp.bfloat16
F32 = jnp.float32

RETURN_SPLIT = (4, 4, 5, 3)


def cost(flops, moved, exps=0):
    return pl.CostEstimate(flops=int(flops), bytes_accessed=int(moved), transcendentals=int(exps))


def dot(a, b):
    return jnp.dot(a, b, preferred_element_type=F32)


def whole(shape):
    zeros = (0,) * len(shape)
    return pl.BlockSpec(shape, lambda *_: zeros, pipeline_mode=pl.Buffered(1))


def xor_blocks(x, axis, me, parts):
    size = x.shape[axis] // parts
    return jnp.concatenate(
        [lax.dynamic_slice_in_dim(x, (me ^ d) * size, size, axis) for d in range(parts)], axis
    )


def after(x, *needed):
    return lax.optimization_barrier((x, needed))[0]


def swap(x, name, size, d):
    return lax.ppermute(x, name, [(i, i ^ d) for i in range(size)])


def exchange(pieces, name, size):
    if len(pieces) != size:
        return [lax.all_to_all(pieces[0], name, split_axis=0, concat_axis=0, tiled=True)]
    order = sorted(range(1, size), key=lambda d: -d)
    got = {d: swap(pieces[d], name, size, d) for d in order}
    return [pieces[0]] + [got[d] for d in range(1, size)]


def inner_kernel(parts, tok, scale, gain, mix, twiddle, *refs):
    outs, rows_of = refs[:parts], refs[parts]
    block = mix.shape[0]
    al = tok.shape[0] // block
    ql = block // parts
    for a in range(al):
        at = pl.ds(a * block, block)
        normed = (tok[at, :].astype(F32) * (gain[...] * scale[at, :])).astype(BF)
        rows_of[at, :] = dot(mix[...], normed) * twiddle[a]
    for d in range(parts):
        for q in range(ql):
            outs[d][q] = rows_of[pl.ds(d * ql + q, al, stride=block), :].astype(BF)


def inner(tokens, scale, gain, mix, twiddle, parts, start, chans):
    count = tokens.shape[0]
    block = mix.shape[0]
    al = count // block
    ql = block // parts
    cb = LANES
    first = start // cb
    return pl.pallas_call(
        lambda *refs: inner_kernel(parts, *refs),
        grid=(chans // cb,),
        in_specs=[
            pl.BlockSpec((count, cb), lambda c: (0, c + first)),
            whole((count, 1)),
            pl.BlockSpec((1, cb), lambda c: (0, c + first)),
            whole((block, block)),
            whole((al, block, 1)),
        ],
        out_specs=[pl.BlockSpec((ql, al, cb), lambda c: (0, 0, c)) for _ in range(parts)],
        out_shape=[jax.ShapeDtypeStruct((ql, al, chans), BF) for _ in range(parts)],
        scratch_shapes=[pltpu.VMEM((count, cb), F32)],
        cost_estimate=cost(2 * count * block * chans, 4 * count * chans),
        name="inner_mix",
    )(tokens, scale, gain, mix, twiddle)


def outer_kernel(parts, sizes, *refs):
    pieces = refs[:parts]
    kern, fwd, back, twiddle = refs[parts : parts + 4]
    outs, rows_of = refs[-1 - len(sizes) : -1], refs[-1]
    width = kern.shape[-1]
    side = twiddle.shape[1]
    pair = fwd.shape[0] // side
    al = side // parts
    for q in range(0, G, pair):
        x = jnp.concatenate([p[q + i] for i in range(pair) for p in pieces], axis=0)
        k = jnp.concatenate([kern[:, q + i].reshape(side, width) for i in range(pair)], axis=0)
        mixed = dot(fwd[...], x).astype(BF)
        filtered = (mixed.astype(F32) * k.astype(F32)).astype(BF)
        backed = dot(back[...], filtered)
        for i in range(pair):
            turned = backed[i * side : (i + 1) * side] * twiddle[q + i]
            for c in range(width // LANES):
                rows_of[c, pl.ds((q + i) * side, side), :] = turned[:, c * LANES : (c + 1) * LANES]
    for d in range(parts):
        r = d * al
        for out, size in zip(outs, sizes, strict=True):
            for i in range(size):
                for c in range(width // LANES):
                    out[d, i, :, c * LANES : (c + 1) * LANES] = rows_of[
                        c, pl.ds(r, G, stride=side), :
                    ].astype(BF)
                r += 1


def outer(pieces, kern, fwd, back, twiddle, sizes, start, chans, carried):
    parts = len(pieces)
    ql, al, width = pieces[0].shape
    side = parts * al
    cb = math.gcd(width, 256)
    first = start // cb
    extra = carried or []
    return pl.pallas_call(
        lambda *refs: outer_kernel(parts, sizes, *refs),
        grid=(width // cb, ql // G),
        in_specs=[pl.BlockSpec((G, al, cb), lambda c, q: (q, 0, c)) for _ in range(parts)]
        + [
            pl.BlockSpec((parts, G, al, cb), lambda c, q: (0, q, 0, c)),
            whole(fwd.shape),
            whole(back.shape),
            pl.BlockSpec((G, side, 1), lambda c, q: (q, 0, 0)),
        ]
        + [pl.BlockSpec(memory_space=pl.ANY) for _ in extra],
        out_specs=[pl.BlockSpec((parts, size, G, cb), lambda c, q: (0, 0, q, c + first)) for size in sizes],
        out_shape=[jax.ShapeDtypeStruct((parts, size, ql, chans), BF) for size in sizes],
        scratch_shapes=[pltpu.VMEM((cb // LANES, G * side, LANES), F32)],
        input_output_aliases={parts + 4 + i: i for i in range(len(extra))},
        cost_estimate=cost(8 * side * side * ql * width, 6 * side * ql * width),
        name="outer_mix",
    )(*pieces, kern, fwd, back, twiddle, *extra)


def eye_at(rows, cols, first):
    return iota((rows, cols), 0) == iota((rows, cols), 1) + first


def places(refs, groups, me):
    return refs if len(refs) == groups else [refs[0].at[me[0] ^ d] for d in range(groups)]


def mix_kernel(groups, me, pieces, tok, scale, gain, gain_two, back, up, mixed_out, *outs):
    outs = places(outs, groups, me)
    block, chans = tok.shape
    conv = dot(back[...], pieces[...].reshape(block, chans))
    wide = tok[...].astype(F32)
    normed = (wide * (gain[...] * scale[...])).astype(BF).astype(F32)
    mixed = wide + conv * (normed / (1.0 + jnp.exp(-normed)))
    mixed_out[...] = mixed
    projected = dot((mixed * gain_two[...]).astype(BF), up[...]).astype(BF)
    width = projected.shape[1] // groups
    sums = jnp.sum(mixed * mixed, axis=1, keepdims=True)
    tail = jnp.zeros((TAIL, width), F32)
    line = iota((TAIL, width), 0)
    for u in range(block // width):
        row = jnp.sum(jnp.where(eye_at(block, width, u * width), sums, 0.0), axis=0, keepdims=True)
        for part in range(3):
            piece = row.astype(BF).astype(F32)
            tail = jnp.where(line == 3 * u + part, piece, tail)
            row = row - piece
    for d in range(groups):
        outs[d][0, :block] = projected[:, d * width : (d + 1) * width]
        outs[d][0, block:] = tail.astype(BF)


def fan(shape, index, groups, stacked):
    if stacked:
        return [pl.BlockSpec((groups,) + shape, lambda t: (0,) + index(t))]
    return [pl.BlockSpec(shape, index) for _ in range(groups)]


def fan_out(shape, groups, stacked):
    if stacked:
        return [jax.ShapeDtypeStruct((groups,) + shape, BF)]
    return [jax.ShapeDtypeStruct(shape, BF) for _ in range(groups)]


SCALAR = pl.BlockSpec(memory_space=pltpu.SMEM)


def mix(me, home, tokens, scale, gain, gain_two, back, up, row, groups, stacked):
    parts, size, ql, chans = home.shape
    block = ql * parts
    count = size * block
    width = up.shape[1] // groups
    return pl.pallas_call(
        lambda *refs: mix_kernel(groups, *refs),
        grid=(size,),
        in_specs=[
            SCALAR,
            pl.BlockSpec((parts, 1, ql, chans), lambda r: (0, r, 0, 0)),
            pl.BlockSpec((block, chans), lambda r: (r + row, 0)),
            pl.BlockSpec((block, 1), lambda r: (r + row, 0)),
            whole((1, chans)),
            whole((1, chans)),
            whole((block, block)),
            whole(up.shape),
        ],
        out_specs=[pl.BlockSpec((block, chans), lambda r: (r, 0))]
        + fan((1, block + TAIL, width), lambda r: (r, 0, 0), groups, stacked),
        out_shape=[jax.ShapeDtypeStruct((count, chans), F32)]
        + fan_out((size, block + TAIL, width), groups, stacked),
        cost_estimate=cost(2 * count * chans * (block + up.shape[1]), 10 * count * chans, count * chans),
        name="mix_tokens",
    )(me, home, tokens, scale, gain, gain_two, back, up)


def hidden_kernel(groups, total, halves, me, up, down, *refs):
    pieces = places(refs[: len(refs) // 2], groups, me)
    outs = places(refs[len(refs) // 2 :], groups, me)
    width = pieces[0].shape[2]
    block = pieces[0].shape[1] - TAIL
    tail = sum(p[0, block:].astype(F32) for p in pieces)
    sums = jnp.zeros((block, 1), F32)
    for u in range(block // width):
        row = tail[3 * u : 3 * u + 1] + tail[3 * u + 1 : 3 * u + 2] + tail[3 * u + 2 : 3 * u + 3]
        sums = sums + jnp.sum(jnp.where(eye_at(block, width, u * width), row, 0.0), axis=1, keepdims=True)
    scale = lax.rsqrt(sums / total + EPS)
    part = width // halves
    inside, middle = up.shape[0] // halves, up.shape[1] // halves
    outside = down.shape[1] // halves
    step = outside // groups
    for h in range(halves):
        x = jnp.concatenate([p[0, :block, h * part : (h + 1) * part] for p in pieces], axis=1)
        up_h = up[h * inside : (h + 1) * inside, h * middle : (h + 1) * middle]
        down_h = down[h * middle : (h + 1) * middle, h * outside : (h + 1) * outside]
        v = dot(x, up_h) * scale
        active = (0.5 * v * (1.0 + jnp.tanh(0.7978845608 * (v + 0.044715 * (v * v * v))))).astype(BF)
        reduced = dot(active, down_h).astype(BF)
        for d in range(groups):
            outs[d][:, h * step : (h + 1) * step] = reduced[:, d * step : (d + 1) * step]


def hidden(me, pieces, up, down, total, halves, groups):
    stacked = len(pieces) != groups
    size, tall, width = pieces[0].shape[-3:]
    block = tall - TAIL
    count = size * block
    step = down.shape[1] // groups
    return pl.pallas_call(
        lambda *refs: hidden_kernel(groups, total, halves, *refs),
        grid=(size,),
        in_specs=[SCALAR, whole(up.shape), whole(down.shape)]
        + fan((1, tall, width), lambda t: (t, 0, 0), groups, stacked),
        out_specs=fan((block, step), lambda t: (t, 0), groups, stacked),
        out_shape=fan_out((count, step), groups, stacked),
        cost_estimate=cost(
            2 * count * up.shape[1] * (up.shape[0] + down.shape[1]) // halves,
            2 * groups * count * (width + step),
            count * up.shape[1],
        ),
        name="hidden_units",
    )(me, up, down, *pieces)


def final_kernel(groups, me, mixed, left, *refs):
    pieces = places(refs[: 1 if len(refs) < groups else groups], groups, me)
    out = refs[-1]
    x = jnp.concatenate([p[...] for p in pieces], axis=1)
    out[...] = (mixed[...] + dot(x, left[...])).astype(BF)


def final(me, pieces, mixed, left, row, count_all, carried, groups):
    stacked = len(pieces) != groups
    count, step = pieces[0].shape[-2:]
    chans = mixed.shape[1]
    tb = min(ROWS, count)
    first = row // tb
    extra = [] if carried is None else [carried]
    return pl.pallas_call(
        lambda *refs: final_kernel(groups, *refs),
        grid=(count // tb,),
        in_specs=[SCALAR, pl.BlockSpec((tb, chans), lambda t: (t, 0)), whole(left.shape)]
        + fan((tb, step), lambda t: (t, 0), groups, stacked)
        + [pl.BlockSpec(memory_space=pl.ANY) for _ in extra],
        out_specs=pl.BlockSpec((tb, chans), lambda t: (t + first, 0)),
        out_shape=jax.ShapeDtypeStruct((count_all, chans), BF),
        input_output_aliases={3 + len(pieces): 0} if extra else {},
        cost_estimate=cost(2 * count * groups * step * chans, 8 * count * chans),
        name="block_out",
    )(me, mixed, left, *pieces, *extra)


def iota(shape, axis):
    return lax.broadcasted_iota(jnp.int32, shape, axis)


def pick(rows, cols, of_col):
    return (iota((rows, cols), 0) == of_col(iota((rows, cols), 1))).astype(BF)


def masked(x, keep):
    rows, cols = iota(x.shape, 0), iota(x.shape, 1)
    return jnp.where(keep(rows, cols), x, 0.0).astype(BF)


def repeat_block(x, times):
    rows, cols = x.shape
    return masked(
        jnp.tile(x.astype(F32), (times, times)), lambda r, c: r // rows == c // cols
    )


def expand_factors(right_up, left_up, right_down, left_down, me, groups, halves):
    il, nj, nk = right_up.shape
    kl, ni, nm = left_up.shape
    nq = right_down.shape[2]
    ql, nkk, nr = left_down.shape
    lk, lr = kl * il, ql * kl

    def place(at, lanes):
        part = lanes // halves
        half, rest = at // (groups * part), at % (groups * part)
        return rest // part, half * part + rest % part

    def up_two_source(r):
        d, lane = place(r, lk)
        return (lane // il) * ni + (me ^ d) * il + lane % il

    def down_one_source(c):
        d, lane = place(c, lr)
        return (me ^ d) * ql + lane % ql

    def down_two_source(r):
        lane = r % lr
        return (lane % ql) * nkk + (me ^ (r // lr)) * kl + lane // ql

    up_one = masked(
        dot(
            right_up.reshape(il * nj, nk),
            pick(nk, groups * lk, lambda c: (me ^ (c // lk)) * kl + c % lk // il),
        ),
        lambda r, c: r // nj == c % il,
    )
    rows = groups * lk
    taken = dot(pick(kl * ni, rows, up_two_source).T, left_up.reshape(kl * ni, nm))
    up_two = masked(
        jnp.tile(taken, (1, kl)), lambda r, c: c // nm == place(r, lk)[1] // il
    )
    down_one = masked(
        dot(right_down.reshape(kl * nm, nq), pick(nq, groups * lr, down_one_source)),
        lambda r, c: r // nm == place(c, lr)[1] // ql,
    )
    rows = groups * lr
    taken = dot(pick(ql * nkk, rows, down_two_source).T, left_down.reshape(ql * nkk, nr)).astype(BF)
    down_two = masked(
        dot(taken, pick(nr, ql * nr, lambda c: c % nr)),
        lambda r, c: c // nr == r % lr % ql,
    )
    return up_one, up_two, down_one, down_two


def splits_of(total, shares):
    unit = total // sum(shares)
    if unit * sum(shares) != total:
        return [total]
    return [unit * share for share in shares]


def make_shards(parts, groups):
    def shards(
        tokens,
        seq_inner,
        seq_outer,
        inv_outer,
        inv_inner,
        twiddle_in,
        twiddle_out,
        freq_kernel,
        first_gain,
        second_gain,
        right_up,
        left_up,
        right_down,
        left_down,
    ):
        _, count, chans = tokens.shape
        total = chans * groups
        block = seq_inner.shape[0]
        ql = block // parts
        al = count // block
        at = lax.axis_index("ctx")
        me = lax.axis_index("hid")
        tok = tokens.reshape(count, chans)

        split = chans // 2 if chans % 512 == 0 else chans
        chan_starts = range(0, chans, split)
        kerns = []
        for c in chan_starts:
            sent = freq_kernel[:, :, c : c + split].reshape(al, parts, ql, split).transpose(1, 2, 0, 3)
            kerns.append(lax.all_to_all(sent, "ctx", split_axis=0, concat_axis=0, tiled=True))

        wide = tok.astype(F32)
        sums = lax.psum(jnp.sum(wide * wide, axis=1), "hid")
        scale = lax.rsqrt(sums / total + EPS).reshape(count, 1)
        gain = first_gain.reshape(1, chans)
        gain_two = second_gain.reshape(1, chans)

        rows_in = xor_blocks(seq_inner, 0, at, parts)
        turn_in = xor_blocks(twiddle_in, 1, at, parts).reshape(al, block, 1)
        waves = [inner(tok, scale, gain, rows_in, turn_in, parts, c, split) for c in chan_starts]
        fwd = repeat_block(xor_blocks(seq_outer, 1, at, parts), 2)
        back = repeat_block(inv_outer, 2)
        turn = twiddle_out.T.reshape(ql, al * parts, 1)
        sizes = splits_of(al, RETURN_SPLIT)
        waves = [exchange(wave, "ctx", parts) for wave in waves]

        lanes = right_up.shape[0] * left_up.shape[0]
        halves = lanes // 128 if lanes % 128 == 0 else 1
        up_one, up_two, down_one, down_two = expand_factors(
            right_up, left_up, right_down, left_down, me, groups, halves
        )
        kerns[0] = after(kerns[0], up_one, up_two, down_one, down_two, turn)
        backed = None
        for f, c in enumerate(chan_starts):
            if f + 1 < len(waves):
                kerns[f] = after(kerns[f], waves[f + 1][-1])
            backed = outer(waves[f], kerns[f], fwd, back, turn, sizes, c, chans, backed)
        chunks = len(sizes)
        place = me.astype(jnp.int32).reshape(1)
        starts = [sum(sizes[:j]) for j in range(chunks)]
        mixed, ups, downs, done, outs = {}, {}, {}, {}, {-1: None}

        def hide(j):
            pieces = ups[j]
            if 1 <= j < chunks - 1:
                pieces = after(pieces, mixed[j + 1])
            if j >= 1:
                pieces = after(pieces, downs[j - 1])
            pieces = hidden(place, pieces, up_two, down_one, total, halves, groups)
            done[j] = pieces
            downs[j] = exchange(pieces, "hid", groups)

        def finish(j):
            outs[j] = final(
                place, downs[j], mixed[j], down_two, starts[j] * block, count, outs[j - 1], groups
            )

        for j in range(chunks):
            needed = []
            if j >= 2:
                needed.append(ups[j - 2])
            if j >= 3:
                needed.append(done[j - 3])
            if j >= 4:
                needed.append(outs[j - 4])
            sent = after(backed[j], *needed) if needed else backed[j]
            home = lax.all_to_all(sent, "ctx", split_axis=0, concat_axis=0, tiled=True)
            mixed[j], *pieces = mix(
                place,
                home,
                tok,
                scale,
                gain,
                gain_two,
                inv_inner,
                up_one,
                starts[j],
                groups,
                j == chunks - 1,
            )
            ups[j] = exchange(pieces, "hid", groups)
            if j >= 1:
                hide(j - 1)
            if j >= 2:
                finish(j - 2)
        hide(chunks - 1)
        for j in range(max(chunks - 2, 0), chunks):
            finish(j)
        return outs[chunks - 1].reshape(1, count, chans)

    return shards


def solution(mesh):
    return jax.shard_map(
        make_shards(mesh.shape["ctx"], mesh.shape["hid"]),
        mesh=mesh,
        in_specs=(
            P(None, "ctx", "hid"),
            P(),
            P(),
            P(),
            P(),
            P("ctx", None),
            P(None, "ctx"),
            P("ctx", None, "hid"),
            P("hid"),
            P("hid"),
            P("hid", None, None),
            P("hid", None, None),
            P("hid", None, None),
            P("hid", None, None),
        ),
        out_specs=P(None, "ctx", "hid"),
        check_vma=False,
    )
```

```python
import math

import jax
import jax.numpy as jnp
from jax import lax
from jax.experimental import pallas as pl
from jax.experimental.pallas import tpu as pltpu
from jax.sharding import PartitionSpec as P

EPS = 1e-06
G = 16
ROWS = 256
TAIL = 16
LANES = 128
BF = jnp.bfloat16
F32 = jnp.float32

RETURN_SPLIT = (5, 4, 4, 3)


def cost(flops, moved, exps=0):
    return pl.CostEstimate(flops=int(flops), bytes_accessed=int(moved), transcendentals=int(exps))


def dot(a, b):
    return jnp.dot(a, b, preferred_element_type=F32)


def whole(shape):
    zeros = (0,) * len(shape)
    return pl.BlockSpec(shape, lambda *_: zeros, pipeline_mode=pl.Buffered(1))


def xor_blocks(x, axis, me, parts):
    size = x.shape[axis] // parts
    return jnp.concatenate(
        [lax.dynamic_slice_in_dim(x, (me ^ d) * size, size, axis) for d in range(parts)], axis
    )


def after(x, *needed):
    return lax.optimization_barrier((x, needed))[0]


def swap(x, name, size, d):
    return lax.ppermute(x, name, [(i, i ^ d) for i in range(size)])


def exchange(pieces, name, size):
    if len(pieces) != size:
        return [lax.all_to_all(pieces[0], name, split_axis=0, concat_axis=0, tiled=True)]
    order = sorted(range(1, size), key=lambda d: -d)
    got = {d: swap(pieces[d], name, size, d) for d in order}
    return [pieces[0]] + [got[d] for d in range(1, size)]


def inner_kernel(parts, tok, scale, gain, mix, twiddle, *refs):
    outs, rows_of = refs[:parts], refs[parts]
    block = mix.shape[0]
    al = tok.shape[0] // block
    ql = block // parts
    for a in range(al):
        at = pl.ds(a * block, block)
        normed = (tok[at, :].astype(F32) * (gain[...] * scale[at, :])).astype(BF)
        rows_of[at, :] = dot(mix[...], normed) * twiddle[a]
    for d in range(parts):
        for q in range(ql):
            outs[d][q] = rows_of[pl.ds(d * ql + q, al, stride=block), :].astype(BF)


def inner(tokens, scale, gain, mix, twiddle, parts, start, chans):
    count = tokens.shape[0]
    block = mix.shape[0]
    al = count // block
    ql = block // parts
    cb = LANES
    first = start // cb
    return pl.pallas_call(
        lambda *refs: inner_kernel(parts, *refs),
        grid=(chans // cb,),
        in_specs=[
            pl.BlockSpec((count, cb), lambda c: (0, c + first)),
            whole((count, 1)),
            pl.BlockSpec((1, cb), lambda c: (0, c + first)),
            whole((block, block)),
            whole((al, block, 1)),
        ],
        out_specs=[pl.BlockSpec((ql, al, cb), lambda c: (0, 0, c)) for _ in range(parts)],
        out_shape=[jax.ShapeDtypeStruct((ql, al, chans), BF) for _ in range(parts)],
        scratch_shapes=[pltpu.VMEM((count, cb), F32)],
        cost_estimate=cost(2 * count * block * chans, 4 * count * chans),
        name="inner_mix",
    )(tokens, scale, gain, mix, twiddle)


def outer_kernel(parts, sizes, *refs):
    pieces = refs[:parts]
    kern, fwd, back, twiddle = refs[parts : parts + 4]
    outs, rows_of = refs[-1 - len(sizes) : -1], refs[-1]
    width = kern.shape[-1]
    side = twiddle.shape[1]
    pair = fwd.shape[0] // side
    al = side // parts
    for q in range(0, G, pair):
        x = jnp.concatenate([p[q + i] for i in range(pair) for p in pieces], axis=0)
        k = jnp.concatenate([kern[:, q + i].reshape(side, width) for i in range(pair)], axis=0)
        mixed = dot(fwd[...], x).astype(BF)
        filtered = (mixed.astype(F32) * k.astype(F32)).astype(BF)
        backed = dot(back[...], filtered)
        for i in range(pair):
            turned = backed[i * side : (i + 1) * side] * twiddle[q + i]
            for c in range(width // LANES):
                rows_of[c, pl.ds((q + i) * side, side), :] = turned[:, c * LANES : (c + 1) * LANES]
    for d in range(parts):
        r = d * al
        for out, size in zip(outs, sizes, strict=True):
            for i in range(size):
                for c in range(width // LANES):
                    out[d, i, :, c * LANES : (c + 1) * LANES] = rows_of[
                        c, pl.ds(r, G, stride=side), :
                    ].astype(BF)
                r += 1


def outer(pieces, kern, fwd, back, twiddle, sizes, start, chans, carried):
    parts = len(pieces)
    ql, al, width = pieces[0].shape
    side = parts * al
    cb = math.gcd(width, 256)
    first = start // cb
    extra = carried or []
    return pl.pallas_call(
        lambda *refs: outer_kernel(parts, sizes, *refs),
        grid=(width // cb, ql // G),
        in_specs=[pl.BlockSpec((G, al, cb), lambda c, q: (q, 0, c)) for _ in range(parts)]
        + [
            pl.BlockSpec((parts, G, al, cb), lambda c, q: (0, q, 0, c)),
            whole(fwd.shape),
            whole(back.shape),
            pl.BlockSpec((G, side, 1), lambda c, q: (q, 0, 0)),
        ]
        + [pl.BlockSpec(memory_space=pl.ANY) for _ in extra],
        out_specs=[pl.BlockSpec((parts, size, G, cb), lambda c, q: (0, 0, q, c + first)) for size in sizes],
        out_shape=[jax.ShapeDtypeStruct((parts, size, ql, chans), BF) for size in sizes],
        scratch_shapes=[pltpu.VMEM((cb // LANES, G * side, LANES), F32)],
        input_output_aliases={parts + 4 + i: i for i in range(len(extra))},
        cost_estimate=cost(8 * side * side * ql * width, 6 * side * ql * width),
        name="outer_mix",
    )(*pieces, kern, fwd, back, twiddle, *extra)


def eye_at(rows, cols, first):
    return iota((rows, cols), 0) == iota((rows, cols), 1) + first


def places(refs, groups, me):
    return refs if len(refs) == groups else [refs[0].at[me[0] ^ d] for d in range(groups)]


def mix_kernel(groups, me, pieces, tok, scale, gain, gain_two, back, up, mixed_out, *outs):
    outs = places(outs, groups, me)
    block, chans = tok.shape
    conv = dot(back[...], pieces[...].reshape(block, chans))
    wide = tok[...].astype(F32)
    normed = (wide * (gain[...] * scale[...])).astype(BF).astype(F32)
    mixed = wide + conv * (normed / (1.0 + jnp.exp(-normed)))
    mixed_out[...] = mixed
    projected = dot((mixed * gain_two[...]).astype(BF), up[...]).astype(BF)
    width = projected.shape[1] // groups
    sums = jnp.sum(mixed * mixed, axis=1, keepdims=True)
    tail = jnp.zeros((TAIL, width), F32)
    line = iota((TAIL, width), 0)
    for u in range(block // width):
        row = jnp.sum(jnp.where(eye_at(block, width, u * width), sums, 0.0), axis=0, keepdims=True)
        for part in range(3):
            piece = row.astype(BF).astype(F32)
            tail = jnp.where(line == 3 * u + part, piece, tail)
            row = row - piece
    for d in range(groups):
        outs[d][0, :block] = projected[:, d * width : (d + 1) * width]
        outs[d][0, block:] = tail.astype(BF)


def fan(shape, index, groups, stacked):
    if stacked:
        return [pl.BlockSpec((groups,) + shape, lambda t: (0,) + index(t))]
    return [pl.BlockSpec(shape, index) for _ in range(groups)]


def fan_out(shape, groups, stacked):
    if stacked:
        return [jax.ShapeDtypeStruct((groups,) + shape, BF)]
    return [jax.ShapeDtypeStruct(shape, BF) for _ in range(groups)]


SCALAR = pl.BlockSpec(memory_space=pltpu.SMEM)


def mix(me, home, tokens, scale, gain, gain_two, back, up, row, groups, stacked):
    parts, size, ql, chans = home.shape
    block = ql * parts
    count = size * block
    width = up.shape[1] // groups
    return pl.pallas_call(
        lambda *refs: mix_kernel(groups, *refs),
        grid=(size,),
        in_specs=[
            SCALAR,
            pl.BlockSpec((parts, 1, ql, chans), lambda r: (0, r, 0, 0)),
            pl.BlockSpec((block, chans), lambda r: (r + row, 0)),
            pl.BlockSpec((block, 1), lambda r: (r + row, 0)),
            whole((1, chans)),
            whole((1, chans)),
            whole((block, block)),
            whole(up.shape),
        ],
        out_specs=[pl.BlockSpec((block, chans), lambda r: (r, 0))]
        + fan((1, block + TAIL, width), lambda r: (r, 0, 0), groups, stacked),
        out_shape=[jax.ShapeDtypeStruct((count, chans), F32)]
        + fan_out((size, block + TAIL, width), groups, stacked),
        cost_estimate=cost(2 * count * chans * (block + up.shape[1]), 10 * count * chans, count * chans),
        name="mix_tokens",
    )(me, home, tokens, scale, gain, gain_two, back, up)


def hidden_kernel(groups, total, halves, me, up, down, *refs):
    pieces = places(refs[: len(refs) // 2], groups, me)
    outs = places(refs[len(refs) // 2 :], groups, me)
    width = pieces[0].shape[2]
    block = pieces[0].shape[1] - TAIL
    tail = sum(p[0, block:].astype(F32) for p in pieces)
    sums = jnp.zeros((block, 1), F32)
    for u in range(block // width):
        row = tail[3 * u : 3 * u + 1] + tail[3 * u + 1 : 3 * u + 2] + tail[3 * u + 2 : 3 * u + 3]
        sums = sums + jnp.sum(jnp.where(eye_at(block, width, u * width), row, 0.0), axis=1, keepdims=True)
    scale = lax.rsqrt(sums / total + EPS)
    part = width // halves
    inside, middle = up.shape[0] // halves, up.shape[1] // halves
    outside = down.shape[1] // halves
    step = outside // groups
    for h in range(halves):
        x = jnp.concatenate([p[0, :block, h * part : (h + 1) * part] for p in pieces], axis=1)
        up_h = up[h * inside : (h + 1) * inside, h * middle : (h + 1) * middle]
        down_h = down[h * middle : (h + 1) * middle, h * outside : (h + 1) * outside]
        v = dot(x, up_h) * scale
        active = (0.5 * v * (1.0 + jnp.tanh(0.7978845608 * (v + 0.044715 * (v * v * v))))).astype(BF)
        reduced = dot(active, down_h).astype(BF)
        for d in range(groups):
            outs[d][:, h * step : (h + 1) * step] = reduced[:, d * step : (d + 1) * step]


def hidden(me, pieces, up, down, total, halves, groups):
    stacked = len(pieces) != groups
    size, tall, width = pieces[0].shape[-3:]
    block = tall - TAIL
    count = size * block
    step = down.shape[1] // groups
    return pl.pallas_call(
        lambda *refs: hidden_kernel(groups, total, halves, *refs),
        grid=(size,),
        in_specs=[SCALAR, whole(up.shape), whole(down.shape)]
        + fan((1, tall, width), lambda t: (t, 0, 0), groups, stacked),
        out_specs=fan((block, step), lambda t: (t, 0), groups, stacked),
        out_shape=fan_out((count, step), groups, stacked),
        cost_estimate=cost(
            2 * count * up.shape[1] * (up.shape[0] + down.shape[1]) // halves,
            2 * groups * count * (width + step),
            count * up.shape[1],
        ),
        name="hidden_units",
    )(me, up, down, *pieces)


def final_kernel(groups, me, mixed, left, *refs):
    pieces = places(refs[: 1 if len(refs) < groups else groups], groups, me)
    out = refs[-1]
    x = jnp.concatenate([p[...] for p in pieces], axis=1)
    out[...] = (mixed[...] + dot(x, left[...])).astype(BF)


def final(me, pieces, mixed, left, row, count_all, carried, groups):
    stacked = len(pieces) != groups
    count, step = pieces[0].shape[-2:]
    chans = mixed.shape[1]
    tb = min(ROWS, count)
    first = row // tb
    extra = [] if carried is None else [carried]
    return pl.pallas_call(
        lambda *refs: final_kernel(groups, *refs),
        grid=(count // tb,),
        in_specs=[SCALAR, pl.BlockSpec((tb, chans), lambda t: (t, 0)), whole(left.shape)]
        + fan((tb, step), lambda t: (t, 0), groups, stacked)
        + [pl.BlockSpec(memory_space=pl.ANY) for _ in extra],
        out_specs=pl.BlockSpec((tb, chans), lambda t: (t + first, 0)),
        out_shape=jax.ShapeDtypeStruct((count_all, chans), BF),
        input_output_aliases={3 + len(pieces): 0} if extra else {},
        cost_estimate=cost(2 * count * groups * step * chans, 8 * count * chans),
        name="block_out",
    )(me, mixed, left, *pieces, *extra)


def iota(shape, axis):
    return lax.broadcasted_iota(jnp.int32, shape, axis)


def pick(rows, cols, of_col):
    return (iota((rows, cols), 0) == of_col(iota((rows, cols), 1))).astype(BF)


def masked(x, keep):
    rows, cols = iota(x.shape, 0), iota(x.shape, 1)
    return jnp.where(keep(rows, cols), x, 0.0).astype(BF)


def repeat_block(x, times):
    rows, cols = x.shape
    return masked(
        jnp.tile(x.astype(F32), (times, times)), lambda r, c: r // rows == c // cols
    )


def expand_factors(right_up, left_up, right_down, left_down, me, groups, halves):
    il, nj, nk = right_up.shape
    kl, ni, nm = left_up.shape
    nq = right_down.shape[2]
    ql, nkk, nr = left_down.shape
    lk, lr = kl * il, ql * kl

    def place(at, lanes):
        part = lanes // halves
        half, rest = at // (groups * part), at % (groups * part)
        return rest // part, half * part + rest % part

    def up_two_source(r):
        d, lane = place(r, lk)
        return (lane // il) * ni + (me ^ d) * il + lane % il

    def down_one_source(c):
        d, lane = place(c, lr)
        return (me ^ d) * ql + lane % ql

    def down_two_source(r):
        lane = r % lr
        return (lane % ql) * nkk + (me ^ (r // lr)) * kl + lane // ql

    up_one = masked(
        dot(
            right_up.reshape(il * nj, nk),
            pick(nk, groups * lk, lambda c: (me ^ (c // lk)) * kl + c % lk // il),
        ),
        lambda r, c: r // nj == c % il,
    )
    rows = groups * lk
    taken = dot(pick(kl * ni, rows, up_two_source).T, left_up.reshape(kl * ni, nm))
    up_two = masked(
        jnp.tile(taken, (1, kl)), lambda r, c: c // nm == place(r, lk)[1] // il
    )
    down_one = masked(
        dot(right_down.reshape(kl * nm, nq), pick(nq, groups * lr, down_one_source)),
        lambda r, c: r // nm == place(c, lr)[1] // ql,
    )
    rows = groups * lr
    taken = dot(pick(ql * nkk, rows, down_two_source).T, left_down.reshape(ql * nkk, nr)).astype(BF)
    down_two = masked(
        dot(taken, pick(nr, ql * nr, lambda c: c % nr)),
        lambda r, c: c // nr == r % lr % ql,
    )
    return up_one, up_two, down_one, down_two


def splits_of(total, shares):
    unit = total // sum(shares)
    if unit * sum(shares) != total:
        return [total]
    return [unit * share for share in shares]


def make_shards(parts, groups):
    def shards(
        tokens,
        seq_inner,
        seq_outer,
        inv_outer,
        inv_inner,
        twiddle_in,
        twiddle_out,
        freq_kernel,
        first_gain,
        second_gain,
        right_up,
        left_up,
        right_down,
        left_down,
    ):
        _, count, chans = tokens.shape
        total = chans * groups
        block = seq_inner.shape[0]
        ql = block // parts
        al = count // block
        at = lax.axis_index("ctx")
        me = lax.axis_index("hid")
        tok = tokens.reshape(count, chans)

        split = chans // 2 if chans % 512 == 0 else chans
        chan_starts = range(0, chans, split)
        kerns = []
        for c in chan_starts:
            sent = freq_kernel[:, :, c : c + split].reshape(al, parts, ql, split).transpose(1, 2, 0, 3)
            kerns.append(lax.all_to_all(sent, "ctx", split_axis=0, concat_axis=0, tiled=True))

        wide = tok.astype(F32)
        sums = lax.psum(jnp.sum(wide * wide, axis=1), "hid")
        scale = lax.rsqrt(sums / total + EPS).reshape(count, 1)
        gain = first_gain.reshape(1, chans)
        gain_two = second_gain.reshape(1, chans)

        rows_in = xor_blocks(seq_inner, 0, at, parts)
        turn_in = xor_blocks(twiddle_in, 1, at, parts).reshape(al, block, 1)
        waves = [inner(tok, scale, gain, rows_in, turn_in, parts, c, split) for c in chan_starts]
        fwd = repeat_block(xor_blocks(seq_outer, 1, at, parts), 2)
        back = repeat_block(inv_outer, 2)
        turn = twiddle_out.T.reshape(ql, al * parts, 1)
        sizes = splits_of(al, RETURN_SPLIT)
        waves = [exchange(wave, "ctx", parts) for wave in waves]

        lanes = right_up.shape[0] * left_up.shape[0]
        halves = lanes // 128 if lanes % 128 == 0 else 1
        up_one, up_two, down_one, down_two = expand_factors(
            right_up, left_up, right_down, left_down, me, groups, halves
        )
        kerns[0] = after(kerns[0], up_one, up_two, down_one, down_two, turn)
        backed = None
        for f, c in enumerate(chan_starts):
            if f + 1 < len(waves):
                kerns[f] = after(kerns[f], waves[f + 1][-1])
            backed = outer(waves[f], kerns[f], fwd, back, turn, sizes, c, chans, backed)
        chunks = len(sizes)
        place = me.astype(jnp.int32).reshape(1)
        starts = [sum(sizes[:j]) for j in range(chunks)]
        mixed, ups, downs, done, outs = {}, {}, {}, {}, {-1: None}

        def hide(j):
            pieces = ups[j]
            if 1 <= j < chunks - 1:
                pieces = after(pieces, mixed[j + 1])
            if j >= 1:
                pieces = after(pieces, downs[j - 1])
            pieces = hidden(place, pieces, up_two, down_one, total, halves, groups)
            done[j] = pieces
            downs[j] = exchange(pieces, "hid", groups)

        def finish(j):
            outs[j] = final(
                place, downs[j], mixed[j], down_two, starts[j] * block, count, outs[j - 1], groups
            )

        for j in range(chunks):
            needed = []
            if j >= 2:
                needed.append(ups[j - 2])
            if j >= 3:
                needed.append(done[j - 3])
            if j >= 4:
                needed.append(outs[j - 4])
            sent = after(backed[j], *needed) if needed else backed[j]
            home = lax.all_to_all(sent, "ctx", split_axis=0, concat_axis=0, tiled=True)
            mixed[j], *pieces = mix(
                place,
                home,
                tok,
                scale,
                gain,
                gain_two,
                inv_inner,
                up_one,
                starts[j],
                groups,
                j == chunks - 1,
            )
            ups[j] = exchange(pieces, "hid", groups)
            if j >= 1:
                hide(j - 1)
            if j >= 2:
                finish(j - 2)
        hide(chunks - 1)
        for j in range(max(chunks - 2, 0), chunks):
            finish(j)
        return outs[chunks - 1].reshape(1, count, chans)

    return shards


def solution(mesh):
    return jax.shard_map(
        make_shards(mesh.shape["ctx"], mesh.shape["hid"]),
        mesh=mesh,
        in_specs=(
            P(None, "ctx", "hid"),
            P(),
            P(),
            P(),
            P(),
            P("ctx", None),
            P(None, "ctx"),
            P("ctx", None, "hid"),
            P("hid"),
            P("hid"),
            P("hid", None, None),
            P("hid", None, None),
            P("hid", None, None),
            P("hid", None, None),
        ),
        out_specs=P(None, "ctx", "hid"),
        check_vma=False,
    )
```
